256 devices in a mesh: segment: 2 (over core), gx: 16 (over x, y), gy: 8 (over z).
Axes of the slice: x: 4, y: 4, z: 8, core: 2. Of those that a mesh axis runs over, the one named last changes fastest.
Arguments:
- volume: bfloat16 [4, 128, 512, 256], P(None, 'gx', 'gy'), may hold values from -6 to 6
- weight_high: bfloat16 [16, 4, 3, 3, 3], replicated, may hold values from -0.625 to 0.625
- bias_high: float32 [16], replicated, may hold values from -3 to 3
- weight_low: bfloat16 [32, 16, 3, 3, 3], replicated, may hold values from -0.3125 to 0.3125
- bias_low: float32 [32], replicated, may hold values from -3 to 3
- head_weight: float32 [32, 4], replicated, may hold values from -3 to 3
- head_bias: float32 [4], replicated, may hold values from -3 to 3
- targets: float32 [4], replicated, may hold values from -8 to 8
Outputs:
- predicted: float32 [4], replicated
- boundary_grad: bfloat16 [16, 64, 256, 128], P(None, 'gx', 'gy')
- grad_weight_high: float32 [16, 4, 3, 3, 3], replicated
- grad_bias_high: float32 [16], replicated
- grad_weight_low: float32 [32, 16, 3, 3, 3], replicated
- grad_bias_low: float32 [32], replicated
- grad_head: float32 [32, 4], replicated
The draws below stay inside these ranges and needn't reach their ends.
All inputs are finite; a program needn't handle non-finite values.
Results may differ from the reference program's by a relative error of at most 0.0054.
Values may be sent and summed in bfloat16 or wider, within the bound.
A program may use at most 192 MiB of HBM per device.

```python
import jax
import jax.numpy as jnp
from jax import lax

CIN = 4
MID = 16
LOW = 32
PARAMS = 4
DEPTH = 256
NX = 128
NY = 512
LOWCELLS = 262144


def shard_levels(stream_key, dims, shards, low, high):
    def one(position, shards_of):
        steps = jax.random.uniform(jax.random.fold_in(jax.random.fold_in(stream_key, 6), position), (shards_of,), jnp.float32, low / len(shards), high / len(shards))
        return jnp.repeat(jnp.exp(steps), dims[position] // shards_of).reshape((-1,) + (1,) * (len(dims) - position - 1))

    loudness = one(*shards[0])
    for cut in shards[1:]:
        loudness = loudness * one(*cut)
    return loudness


def noise(rng, dims, scale, limit, cuts=(), dtype=jnp.bfloat16):
    loudness = shard_levels(rng, dims, cuts, -0.22, 0.18) if cuts else 1.0
    entries = jax.random.normal(rng, dims, jnp.float32) * scale * loudness
    return jnp.minimum(jnp.maximum(entries, -limit), limit).astype(dtype)


def setup_inputs(seed: int = 0) -> dict:
    key_list = jax.random.split(jax.random.key(seed), 9)
    return {
        "volume": noise(key_list[0], (CIN, NX, NY, DEPTH), 1.0, 6.0, ((1, 16), (2, 8))),
        "weight_high": noise(key_list[1], (MID, CIN, 3, 3, 3), (27 * CIN) ** -0.5, 0.625),
        "bias_high": noise(key_list[2], (MID,), 0.5, 3.0, (), jnp.float32),
        "weight_low": noise(key_list[3], (LOW, MID, 3, 3, 3), (27 * MID) ** -0.5, 0.3125),
        "bias_low": noise(key_list[4], (LOW,), 0.5, 3.0, (), jnp.float32),
        "head_weight": noise(key_list[5], (LOW, PARAMS), 0.5, 3.0, (), jnp.float32),
        "head_bias": noise(key_list[6], (PARAMS,), 0.5, 3.0, (), jnp.float32),
        "targets": noise(key_list[7], (PARAMS,), 2.0, 8.0, (), jnp.float32),
    }


layout_spec = ('NCDHW', 'OIDHW', 'NCDHW')

def conv_down(widened, weight):
    return lax.conv_general_dilated(widened[None], weight, (2, 2, 2), 'VALID', dimension_numbers=layout_spec, precision=lax.Precision.HIGHEST)[0]

def lower_pad(block):
    return jnp.pad(block, ((0, 0), (1, 0), (1, 0), (1, 0)))

def silu_slope(values):
    sigmoid_part = jax.nn.sigmoid(values)
    return sigmoid_part * (1.0 + values * (1.0 - sigmoid_part))

def tap_grad(widened, upstream):
    out_chans, size_x, size_y, size_z = upstream.shape
    in_chans = widened.shape[0]
    collected = []
    for first_tap in range(3):
        for second_tap in range(3):
            for third_tap in range(3):
                window = lax.slice(widened, (0, first_tap, second_tap, third_tap), (in_chans, first_tap + 2 * size_x - 1, second_tap + 2 * size_y - 1, third_tap + 2 * size_z - 1), (1, 2, 2, 2))
                collected.append(jnp.einsum('opqr,ipqr->oi', upstream, window, precision=lax.Precision.HIGHEST))
    return jnp.stack(collected, axis=-1).reshape(out_chans, in_chans, 3, 3, 3)

def tap_data(upstream, weight, in_chans):
    out_chans, size_x, size_y, size_z = upstream.shape
    result = jnp.zeros((in_chans, 2 * size_x + 1, 2 * size_y + 1, 2 * size_z + 1), jnp.float32)
    for first_tap in range(3):
        for second_tap in range(3):
            for third_tap in range(3):
                piece = jnp.einsum('opqr,oi->ipqr', upstream, weight[:, :, first_tap, second_tap, third_tap], precision=lax.Precision.HIGHEST)
                result = result.at[:, first_tap:first_tap + 2 * size_x - 1:2, second_tap:second_tap + 2 * size_y - 1:2, third_tap:third_tap + 2 * size_z - 1:2].add(piece)
    return result

def reference(volume, weight_high, bias_high, weight_low, bias_low, head_weight, head_bias, targets):
    widened_high = lower_pad(volume.astype(jnp.float32))
    pre_high = conv_down(widened_high, weight_high.astype(jnp.float32)) + bias_high[:, None, None, None]
    act_high = jax.nn.silu(pre_high).astype(jnp.bfloat16)
    widened_low = lower_pad(act_high.astype(jnp.float32))
    pre_low = conv_down(widened_low, weight_low.astype(jnp.float32)) + bias_low[:, None, None, None]
    pooled = lax.optimization_barrier(jnp.sum(jax.nn.silu(pre_low), axis=(1, 2, 3))) / LOWCELLS
    predicted = jnp.dot(pooled, head_weight, precision=lax.Precision.HIGHEST) + head_bias
    error = predicted - targets
    grad_head = pooled[:, None] * error[None, :]
    signal = jnp.dot(head_weight, error, precision=lax.Precision.HIGHEST)
    up_low = (signal[:, None, None, None] * silu_slope(pre_low)).astype(jnp.bfloat16)
    up_low_wide = up_low.astype(jnp.float32)
    grad_weight_low = tap_grad(widened_low, up_low_wide) / LOWCELLS
    grad_bias_low = lax.optimization_barrier(jnp.sum(up_low_wide, axis=(1, 2, 3))) / LOWCELLS
    spread = tap_data(up_low_wide, weight_low.astype(jnp.float32), MID)
    boundary_grad = spread[:, 1:, 1:, 1:].astype(jnp.bfloat16)
    up_high = (boundary_grad.astype(jnp.float32) * silu_slope(pre_high)).astype(jnp.bfloat16)
    up_high_wide = up_high.astype(jnp.float32)
    grad_weight_high = tap_grad(widened_high, up_high_wide) / LOWCELLS
    grad_bias_high = lax.optimization_barrier(jnp.sum(up_high_wide, axis=(1, 2, 3))) / LOWCELLS
    return (predicted, boundary_grad, grad_weight_high, grad_bias_high, grad_weight_low, grad_bias_low, grad_head)
```

```python
import functools

import jax
import jax.numpy as jnp
import numpy as np
from jax import lax
from jax.experimental import pallas as pl
from jax.experimental.pallas import tpu as pltpu
from jax.sharding import PartitionSpec as P

MESH = pl.DeviceIdType.MESH
BF = jnp.bfloat16
F32 = jnp.float32


def depth_taps():
    z = np.arange(256)[:, None, None]
    k = np.arange(3)[None, :, None]
    p = np.arange(128)[None, None, :]
    return (z == 2 * p + k - 1).reshape(256, 384)


def rows_to_channels():
    out = np.zeros((16, 16, 12, 16), bool)
    for r in range(12):
        for y in range(16):
            out[y, r, r, y] = True
    return out.reshape(256, 192)


def depth_taps_low():
    out = np.zeros((2, 128, 3, 2, 64), bool)
    for h in range(2):
        for k in range(3):
            for p in range(64):
                if 2 * p + k - 1 >= 0:
                    out[h, 2 * p + k - 1, k, h, p] = True
    return out.reshape(256, 384)


def depth_spread():
    out = np.zeros((2, 64, 2, 3, 128), bool)
    for h in range(2):
        for k in range(3):
            for p in range(64):
                if 2 * p + k - 1 >= 0:
                    out[h, p, h, k, 2 * p + k - 1] = True
    return out.reshape(128, 768)


def channels_to_rows():
    out = np.zeros((16, 16, 16, 16), bool)
    for i in range(16):
        for y in range(16):
            out[i, y, y, i] = True
    return out.reshape(256, 256)


def mm(a, b):
    return lax.dot_general(a, b, (((1,), (0,)), ((), ())), preferred_element_type=F32)


def mm_nt(a, b):
    return lax.dot_general(a, b, (((1,), (1,)), ((), ())), preferred_element_type=F32)


def kernel(
    nx, ny, cells,
    v, w1, b1, wl, bl, hw, hb, tg, wb, s1, p1, s2, e1, p2,
    bg_out, pred_out, head_out, grad_out,
    halo, a1, pre, act, taps, slope, slope_y, up, grad_b,
    pool_s, pool_1, pool_2, gsend, g_1, g_2s, g_2, g_3,
    hs, hr, p1s, p1r, p2s, p2r, g1s, g1r, g2s, g2r, g3s, g3r,
):
    mx = lax.axis_index("gx")
    my = lax.axis_index("gy")
    xu, xd = lax.rem(mx + 1, nx), lax.rem(mx + nx - 1, nx)
    yu, yd = lax.rem(my + 1, ny), lax.rem(my + ny - 1, ny)

    barrier = pltpu.get_barrier_semaphore()
    partners = [{"gx": lax.rem(mx + d, nx)} for d in range(1, nx)]
    partners += [{"gy": lax.rem(my + d, ny)} for d in range(1, ny)]
    partners += [{"gx": xu, "gy": yu}, {"gx": xd, "gy": yd}]
    for peer in partners:
        pl.semaphore_signal(barrier, inc=1, device_id=peer, device_id_type=MESH)
    pl.semaphore_wait(barrier, len(partners))

    def send(n, src, dst, peer):
        copy = pltpu.make_async_remote_copy(
            src_ref=src, dst_ref=dst, send_sem=hs.at[n], recv_sem=hr.at[n],
            device_id=peer, device_id_type=MESH,
        )
        copy.start()
        return copy

    copies = []
    c_raw = send(0, v.at[:, 7], halo, {"gx": xu})
    copies.append(c_raw)

    def to_channels(load, xs, yb):
        parts = []
        for h in range(2):
            raw = load(yb * 2 + h).reshape(64, 256)
            d = mm(raw, s1[...]).astype(BF)
            parts.append(jnp.concatenate([d[:, 0:128], d[:, 128:256], d[:, 256:384]], axis=0))
        out = mm(p1[...], jnp.concatenate(parts, axis=1)).astype(BF)
        for h in range(2):
            start = pl.multiple_of(16 + (yb * 2 + h) * 256, 16)
            a1[xs, pl.ds(start, 256), :] = out[:, h * 128:(h + 1) * 128]

    def own_plane(t, carry):
        x, yb = t // 2, lax.rem(t, 2)

        def load(b):
            return v[:, x, pl.ds(pl.multiple_of(b * 16, 16), 16), :]

        to_channels(load, x + 1, yb)
        return carry

    lax.fori_loop(0, 16, own_plane, 0)

    c_a1y = send(1, a1.at[pl.ds(1, 8), pl.ds(1024, 16)], a1.at[pl.ds(1, 8), pl.ds(0, 16)], {"gy": yu})
    c_a1c = send(2, a1.at[8, pl.ds(1024, 16)], a1.at[0, pl.ds(0, 16)], {"gx": xu, "gy": yu})
    copies += [c_a1y, c_a1c]

    c_raw.wait_recv()

    @pl.when(mx == 0)
    def _():
        halo[...] = jnp.zeros_like(halo)

    def halo_plane(yb, carry):
        def load(b):
            return halo[:, pl.ds(pl.multiple_of(b * 16, 16), 16), :]

        to_channels(load, 0, yb)
        return carry

    lax.fori_loop(0, 2, halo_plane, 0)
    c_a1y.wait_recv()
    c_a1c.wait_recv()

    @pl.when(my == 0)
    def _():
        a1[:, pl.ds(0, 16), :] = jnp.zeros((9, 16, 128), BF)

    @pl.when(mx == 0)
    def _():
        a1[0, pl.ds(0, 16), :] = jnp.zeros((16, 128), BF)

    def conv_high(t, carry):
        xp, yp = t // 16, lax.rem(t, 16)
        cols = []
        for h in range(2):
            px = xp * 2 + h
            start = pl.multiple_of(yp * 64, 16)
            cols.append(jnp.concatenate([a1[2 * px + k, pl.ds(start, 80), :] for k in range(3)], axis=0))
        out = mm(w1[...], jnp.concatenate(cols, axis=1)) + b1[...]
        sig = jax.nn.sigmoid(out)
        acts = (out * sig).astype(BF)
        for h in range(2):
            px = xp * 2 + h
            pre[px, pl.ds(pl.multiple_of(yp * 32, 32), 32), :] = out[:, h * 128:(h + 1) * 128]
            act[px + 1, pl.ds(pl.multiple_of(16 + yp * 32, 16), 32), :] = acts[:, h * 128:(h + 1) * 128]
        return carry

    lax.fori_loop(0, 32, conv_high, 0)

    c_ax = send(3, act.at[4, pl.ds(16, 512)], act.at[0, pl.ds(16, 512)], {"gx": xu})
    c_ay = send(4, act.at[pl.ds(1, 4), pl.ds(512, 16)], act.at[pl.ds(1, 4), pl.ds(0, 16)], {"gy": yu})
    c_ac = send(5, act.at[4, pl.ds(512, 16)], act.at[0, pl.ds(0, 16)], {"gx": xu, "gy": yu})
    copies += [c_ax, c_ay, c_ac]
    c_ax.wait_recv()
    c_ay.wait_recv()
    c_ac.wait_recv()

    @pl.when(mx == 0)
    def _():
        act[0] = jnp.zeros((528, 128), BF)

    @pl.when(my == 0)
    def _():
        act[:, pl.ds(0, 16), :] = jnp.zeros((5, 16, 128), BF)

    def to_taps(xs, carry):
        for first, count in ((0, 4), (4, 4), (8, 4), (12, 5)):
            low = act[xs, 16 * first:16 * (first + count), :]
            high = act[xs, 256 + 16 * first:256 + 16 * (first + count), :]
            d = mm(jnp.concatenate([low, high], axis=1), s2[...]).astype(BF)
            for t in range(count):
                for k in range(3):
                    row = ((first + t) * 3 + k) * 16
                    taps[xs, row:row + 16, :] = d[16 * t:16 * (t + 1), 128 * k:128 * (k + 1)]
        return carry

    lax.fori_loop(0, 5, to_taps, 0)

    def window(px, j):
        start = pl.multiple_of(j * 96, 16)
        return jnp.concatenate([taps[2 * px + k, pl.ds(start, 144), :] for k in range(3)], axis=0)

    def conv_low(j, total):
        out = mm(wl[...], jnp.concatenate([window(0, j), window(1, j)], axis=1)) + bl[...]
        sig = jax.nn.sigmoid(out)
        slopes = sig * (1.0 + out * (1.0 - sig))
        values = out * sig
        for px in range(2):
            slope[px, pl.ds(pl.multiple_of(j * 32, 32), 32), :] = slopes[:, px * 128:(px + 1) * 128]
        return total + values[:, :128] + values[:, 128:]

    total = lax.fori_loop(0, 8, conv_low, jnp.zeros((32, 128), F32))

    c_sx = send(6, slope.at[0], slope.at[2], {"gx": xd})
    c_sy = send(7, slope.at[pl.ds(0, 2), pl.ds(0, 32)], slope_y.at[pl.ds(0, 2)], {"gy": yd})
    c_sc = send(8, slope.at[0, pl.ds(0, 32)], slope_y.at[2], {"gx": xd, "gy": yd})
    copies += [c_sx, c_sy, c_sc]

    lane = lax.broadcasted_iota(jnp.int32, (32, 128), 1)
    row = lax.broadcasted_iota(jnp.int32, (32, 128), 0)
    sums = jnp.sum(total, axis=1, keepdims=True)
    flat = jnp.sum(jnp.where(lane == row, sums, 0.0), axis=0, keepdims=True)
    mine = jnp.broadcast_to(flat, (8, 128))

    def exchange(axis, me, n, buffer, source, ssem, rsem):
        out = []
        for d in range(1, n):
            peer = lax.rem(me + d, n)
            copy = pltpu.make_async_remote_copy(
                src_ref=source(peer), dst_ref=buffer.at[me], send_sem=ssem.at[peer], recv_sem=rsem.at[me],
                device_id={axis: peer}, device_id_type=MESH,
            )
            copy.start()
            out.append(copy)
        return out

    def arrive(me, n, buffer, rsem):
        for d in range(1, n):
            peer = lax.rem(me + d, n)
            pltpu.make_async_copy(buffer.at[peer], buffer.at[peer], rsem.at[peer]).wait()

    pool_s[0] = mine
    pool_1[mx] = mine
    copies += exchange("gx", mx, nx, pool_1, lambda peer: pool_s.at[0], p1s, p1r)

    def slope_high(t, carry):
        px, yp = t // 8, lax.rem(t, 8)
        at = pl.ds(pl.multiple_of(yp * 64, 64), 64)
        val = pre[px, at, :]
        sig = jax.nn.sigmoid(val)
        pre[px, at, :] = sig * (1.0 + val * (1.0 - sig))
        return carry

    lax.fori_loop(0, 32, slope_high, 0)

    arrive(mx, nx, pool_1, p1r)
    part = pool_1[0]
    for d in range(1, nx):
        part = part + pool_1[d]
    pool_s[1] = part
    pool_2[my] = part
    copies += exchange("gy", my, ny, pool_2, lambda peer: pool_s.at[1], p2s, p2r)
    arrive(my, ny, pool_2, p2r)
    part = pool_2[0]
    for d in range(1, ny):
        part = part + pool_2[d]
    pooled = jnp.sum(jnp.where(lane == row, part[0:1, :], 0.0), axis=1, keepdims=True) * (1.0 / cells)
    weight = hw[...]
    predicted = jnp.sum(pooled * weight, axis=0, keepdims=True) + hb[...]
    error = predicted - tg[...]
    pred_out[...] = predicted
    head_out[...] = pooled * error
    signal = jnp.sum(weight * error, axis=1, keepdims=True)

    c_sx.wait_recv()
    c_sy.wait_recv()
    c_sc.wait_recv()

    @pl.when(mx == nx - 1)
    def _():
        slope[2] = jnp.zeros((256, 128), F32)
        slope_y[2] = jnp.zeros((32, 128), F32)

    @pl.when(my == ny - 1)
    def _():
        slope_y[...] = jnp.zeros((3, 32, 128), F32)

    def low_back(j, carry):
        g, gb = carry
        for px in range(3):
            f = signal * slope[px, pl.ds(pl.multiple_of(j * 32, 32), 32), :]
            u = f.astype(BF)
            if px < 2:
                g = g + mm_nt(u, window(px, j))
                gb = gb + u.astype(F32)
            d = mm(u, e1[...]).astype(BF)
            for h in range(2):
                for k in range(3):
                    start = pl.multiple_of(((8 * h + j) * 3 + k) * 32, 32)
                    col = (h * 3 + k) * 128
                    up[px, pl.ds(start, 32), :] = d[:, col:col + 128]
        return g, gb

    g_low, gb_low = lax.fori_loop(0, 8, low_back, (jnp.zeros((32, 432), F32), jnp.zeros((32, 128), F32)))
    for px in range(3):
        u = (signal * slope_y[px]).astype(BF)
        d = mm(u, e1[:, 0:384]).astype(BF)
        for k in range(3):
            up[px, (48 + k) * 32:(49 + k) * 32, :] = d[:, k * 128:(k + 1) * 128]

    def high_back(t, carry):
        g, gb = carry
        ax, ay = t // 16, lax.rem(t, 16)
        start = pl.multiple_of(ay * 96, 32)
        rhs = jnp.concatenate([up[ax, pl.ds(start, 192), :], up[ax + 1, pl.ds(start, 192), :]], axis=0)
        out = mm(wb[...], rhs).astype(BF)
        at = pl.ds(pl.multiple_of(ay * 32, 32), 32)
        ws, ups = [], []
        for sx in range(2):
            qx = 2 * ax + sx
            tile = out[32 * sx:32 * (sx + 1), :]
            grad_b[qx, at, :] = tile
            u = (tile.astype(F32) * pre[qx, at, :]).astype(BF)
            gb = gb + u.astype(F32)
            ups.append(u)
            begin = pl.multiple_of(ay * 64, 16)
            ws.append(jnp.concatenate([a1[2 * qx + k, pl.ds(begin, 80), :] for k in range(3)], axis=0))
        g = g + mm_nt(jnp.concatenate(ups, axis=1), jnp.concatenate(ws, axis=1))
        return g, gb

    g_high, gb_high = lax.fori_loop(0, 32, high_back, (jnp.zeros((32, 240), F32), jnp.zeros((32, 128), F32)))

    scale = 1.0 / cells
    pieces = []
    for k in range(3):
        pieces.append(g_high[0:16, k * 80:k * 80 + 48] + g_high[16:32, k * 80 + 32:k * 80 + 80])
    g_w = jnp.concatenate(pieces, axis=1)
    halves = jnp.concatenate([g_w[:, 0:72], g_w[:, 72:144]], axis=0)
    bias_low = jnp.sum(gb_low, axis=1, keepdims=True)
    bias_high = jnp.sum(gb_high, axis=1, keepdims=True)
    last = jnp.concatenate(
        [g_low[:, 384:432], halves, bias_low, bias_high, jnp.zeros((32, 6), F32)], axis=1
    )
    blocks = [g_low[:, 0:128], g_low[:, 128:256], g_low[:, 256:384], last]
    for b in range(4):
        for c in range(4):
            gsend[b * 4 + c] = blocks[c][8 * b:8 * (b + 1), :] * scale

    per = 16 // nx
    g_1[mx] = gsend[pl.ds(mx * per, per)]
    copies += exchange("gx", mx, nx, g_1, lambda peer: gsend.at[pl.ds(peer * per, per)], g1s, g1r)

    def place(t, carry):
        qx = t // 2
        h = lax.rem(t, 2)
        block = grad_b[qx, pl.ds(pl.multiple_of(h * 256, 256), 256), :]
        out = mm(p2[...], block).astype(BF).reshape(16, 16, 128)
        bg_out[:, qx, pl.ds(pl.multiple_of(h * 16, 16), 16), :] = out
        return carry

    lax.fori_loop(0, 8, place, 0)

    arrive(mx, nx, g_1, g1r)
    part = g_1[0]
    for d in range(1, nx):
        part = part + g_1[d]
    g_2s[...] = part
    g_2[my] = part
    copies += exchange("gy", my, ny, g_2, lambda peer: g_2s, g2s, g2r)
    arrive(my, ny, g_2, g2r)
    part = g_2[0]
    for d in range(1, ny):
        part = part + g_2[d]
    g_3[mx] = part
    copies += exchange("gx", mx, nx, g_3, lambda peer: g_3.at[mx], g3s, g3r)
    arrive(mx, nx, g_3, g3r)
    for d in range(nx):
        grad_out[pl.ds(d * per, per)] = g_3[d]
    for copy in copies:
        copy.wait_send()


def shards(nx, ny, volume, weight_high, bias_high, weight_low, bias_low, head_weight, head_bias, targets):
    cells = 2 * nx * 16 * ny * 64
    wh = jnp.transpose(weight_high, (0, 2, 3, 4, 1))
    wh = jnp.pad(wh, ((0, 0), (0, 0), (0, 0), (0, 1), (0, 0))).reshape(16, 3, 3, 16)
    w1 = jnp.concatenate(
        [
            jnp.pad(wh, ((0, 0), (0, 0), (0, 2), (0, 0))).reshape(16, 240),
            jnp.pad(wh, ((0, 0), (0, 0), (2, 0), (0, 0))).reshape(16, 240),
        ],
        axis=0,
    )
    wl = jnp.transpose(weight_low, (0, 2, 3, 4, 1)).reshape(32, 432)
    wt = jnp.transpose(weight_low, (1, 2, 3, 4, 0))
    wt = jnp.pad(wt, ((0, 0), (0, 1), (0, 1), (0, 0), (0, 0)))
    tap = ((1, 3), (2, 0))
    wb = jnp.stack(
        [
            jnp.stack([wt[:, tap[sx][dx], tap[sy][dy]] for dx in range(2) for dy in range(2)], axis=1)
            for sx in range(2)
            for sy in range(2)
        ],
        axis=0,
    ).reshape(64, 384)
    b1 = jnp.concatenate([bias_high, bias_high])[:, None]
    tables = [jnp.asarray(t().astype(np.float32), BF) for t in (depth_taps, rows_to_channels, depth_taps_low, depth_spread, channels_to_rows)]
    vm = pl.BlockSpec(memory_space=pltpu.VMEM)
    dma = pltpu.SemaphoreType.DMA
    per = 16 // nx
    bg, pred, head, grads = pl.pallas_call(
        functools.partial(kernel, nx, ny, cells),
        out_shape=(
            jax.ShapeDtypeStruct((16, 4, 32, 128), BF),
            jax.ShapeDtypeStruct((1, 4), F32),
            jax.ShapeDtypeStruct((32, 4), F32),
            jax.ShapeDtypeStruct((16, 8, 128), F32),
        ),
        in_specs=[vm] * 14,
        out_specs=(vm,) * 4,
        scratch_shapes=[
            pltpu.VMEM((4, 64, 256), BF),
            pltpu.VMEM((9, 1040, 128), BF),
            pltpu.VMEM((4, 512, 128), F32),
            pltpu.VMEM((5, 528, 128), BF),
            pltpu.VMEM((5, 816, 128), BF),
            pltpu.VMEM((3, 256, 128), F32),
            pltpu.VMEM((3, 32, 128), F32),
            pltpu.VMEM((3, 1632, 128), BF),
            pltpu.VMEM((4, 512, 128), BF),
            pltpu.VMEM((2, 8, 128), F32),
            pltpu.VMEM((nx, 8, 128), F32),
            pltpu.VMEM((ny, 8, 128), F32),
            pltpu.VMEM((16, 8, 128), F32),
            pltpu.VMEM((nx, per, 8, 128), F32),
            pltpu.VMEM((per, 8, 128), F32),
            pltpu.VMEM((ny, per, 8, 128), F32),
            pltpu.VMEM((nx, per, 8, 128), F32),
            dma((9,)), dma((9,)),
            dma((nx,)), dma((nx,)), dma((ny,)), dma((ny,)),
            dma((nx,)), dma((nx,)), dma((ny,)), dma((ny,)), dma((nx,)), dma((nx,)),
        ],
        compiler_params=pltpu.CompilerParams(
            collective_id=0, has_side_effects=True, vmem_limit_bytes=48 << 20
        ),
        name="fused",
    )(
        volume, w1, b1, wl, bias_low[:, None], head_weight, head_bias[None], targets[None], wb, *tables
    )
    g = grads.reshape(4, 4, 8, 128).transpose(0, 2, 1, 3).reshape(32, 512)
    g_low = g[:, :432].reshape(32, 27, 16).transpose(0, 2, 1).reshape(32, 16, 3, 3, 3)
    g_high = jnp.concatenate([g[:16, 432:504], g[16:, 432:504]], axis=1).reshape(16, 3, 3, 4, 4)[:, :, :, :3]
    g_high = g_high.transpose(0, 4, 1, 2, 3)
    gb_low = g[:, 504]
    gb_high = g[:16, 505] + g[16:, 505]
    return pred[0], bg, g_high, gb_high, g_low, gb_low, head


def solution(mesh):
    nx, ny = mesh.shape["gx"], mesh.shape["gy"]
    placed = (P(None, "gx", "gy", None), P(), P(), P(), P(), P(), P(), P())
    return jax.shard_map(
        functools.partial(shards, nx, ny),
        mesh=mesh,
        in_specs=placed,
        out_specs=(P(), P(None, "gx", "gy", None), P(), P(), P(), P(), P()),
        check_vma=False,
    )
```

```python
import functools

import jax
import jax.numpy as jnp
import numpy as np
from jax import lax
from jax.experimental import pallas as pl
from jax.experimental.pallas import tpu as pltpu
from jax.sharding import PartitionSpec as P

MESH = pl.DeviceIdType.MESH
BF = jnp.bfloat16
F32 = jnp.float32
UNROLL = (1,) * 10


def depth_taps():
    z = np.arange(256)[:, None, None]
    k = np.arange(3)[None, :, None]
    p = np.arange(128)[None, None, :]
    return (z == 2 * p + k - 1).reshape(256, 384)


def rows_to_channels():
    out = np.zeros((16, 16, 12, 16), bool)
    for r in range(12):
        for y in range(16):
            out[y, r, r, y] = True
    return out.reshape(256, 192)


def depth_taps_low():
    out = np.zeros((2, 128, 3, 2, 64), bool)
    for h in range(2):
        for k in range(3):
            for p in range(64):
                if 2 * p + k - 1 >= 0:
                    out[h, 2 * p + k - 1, k, h, p] = True
    return out.reshape(256, 384)


def depth_spread():
    out = np.zeros((2, 64, 2, 3, 128), bool)
    for h in range(2):
        for k in range(3):
            for p in range(64):
                if 2 * p + k - 1 >= 0:
                    out[h, p, h, k, 2 * p + k - 1] = True
    return out.reshape(128, 768)


def channels_to_rows():
    out = np.zeros((16, 16, 16, 16), bool)
    for i in range(16):
        for y in range(16):
            out[i, y, y, i] = True
    return out.reshape(256, 256)


def low_order():
    out = np.zeros((512, 432), bool)
    for t in range(27):
        for i in range(16):
            out[t * 16 + i, i * 27 + t] = True
    return out


def high_order():
    out = np.zeros((2, 3, 5, 16, 128), bool)
    for s in range(2):
        for kx in range(3):
            for ky in range(3):
                for kz in range(3):
                    for c in range(4):
                        out[s, kx, ky + 2 * s, kz * 4 + c, c * 27 + kx * 9 + ky * 3 + kz] = True
    return out.reshape(2, 240, 128)


def mm(a, b):
    return lax.dot_general(a, b, (((1,), (0,)), ((), ())), preferred_element_type=F32)


def mm_nt(a, b):
    return lax.dot_general(a, b, (((1,), (1,)), ((), ())), preferred_element_type=F32)


def thirds(x):
    a = x.astype(BF)
    rest = x - a.astype(F32)
    b = rest.astype(BF)
    c = (rest - b.astype(F32)).astype(BF)
    return jnp.concatenate([a, b, c], axis=0)


def select(x, table):
    n = x.shape[0]
    out = mm(thirds(x), table)
    return out[0:n] + out[n:2 * n] + out[2 * n:3 * n]


def sigmoid(x):
    return jax.nn.sigmoid(x)


def kernel(
    nx, ny, cells,
    v, w1, b1, wl, bl, hw, hb, tg, wb, s1, p1, s2, e1, p2, ol, oh,
    bg_out, pred_out, head_out, low_out, low_bias, high_out,
    halo, a1, pre, act, taps, slope, slope_y, up, grad_b,
    pool_s, pool_1, pool_2, gsend, g_1, g_2s, g_2, g_3, h_s, h_1, h_2,
    hs, hr, ss, rs,
):
    sg = lax.axis_index("segment")
    mx = lax.axis_index("gx")
    my = lax.axis_index("gy")
    group = 2 * ny
    mg = sg * ny + my
    yu, yd = lax.rem(my + 1, ny), lax.rem(my + ny - 1, ny)
    xu = {"segment": 1 - sg, "gx": lax.rem(mx + sg, nx)}
    xd = {"segment": 1 - sg, "gx": lax.rem(mx + nx - 1 + sg, nx)}
    first_x = jnp.logical_and(mx == 0, sg == 0)
    last_x = jnp.logical_and(mx == nx - 1, sg == 1)

    def column(d):
        return {"gx": lax.rem(mx + d, nx)}

    def member(d):
        at = lax.rem(mg + d, group)
        return {"segment": at // ny, "gy": lax.rem(at, ny)}

    barrier = pltpu.get_barrier_semaphore()
    partners = [column(d) for d in range(1, nx)] + [member(d) for d in range(1, group)]
    partners += [xu, xd, {**xu, "gy": yu}, {**xd, "gy": yd}]
    for peer in partners:
        pl.semaphore_signal(barrier, inc=1, device_id=peer, device_id_type=MESH)

    copies = []

    def send(n, src, dst, peer):
        copy = pltpu.make_async_remote_copy(
            src_ref=src, dst_ref=dst, send_sem=hs.at[n], recv_sem=hr.at[n],
            device_id=peer, device_id_type=MESH,
        )
        copy.start()
        copies.append(copy)
        return copy

    stages = []

    def spread(stage, n, me, to, buffer, source):
        for d in range(1, n):
            pltpu.make_async_remote_copy(
                src_ref=source(lax.rem(me + d, n)), dst_ref=buffer.at[me],
                send_sem=ss.at[stage], recv_sem=rs.at[stage],
                device_id=to(d), device_id_type=MESH,
            ).start()
        stages.append((stage, buffer, n))

    def arrive(stage, buffer, n):
        ref = buffer.at[pl.ds(0, n - 1)]
        pltpu.make_async_copy(ref, ref, rs.at[stage]).wait()

    def add_up(buffer, n):
        part = buffer[0]
        for d in range(1, n):
            part = part + buffer[d]
        return part

    def to_channels(load, xs, yb):
        parts = []
        for h in range(2):
            raw = load(yb * 2 + h).reshape(64, 256)
            d = mm(raw, s1[...]).astype(BF)
            parts.append(jnp.concatenate([d[:, 0:128], d[:, 128:256], d[:, 256:384]], axis=0))
        out = mm(p1[...], jnp.concatenate(parts, axis=1)).astype(BF)
        for h in range(2):
            start = pl.multiple_of(16 + (yb * 2 + h) * 256, 16)
            a1[xs, pl.ds(start, 256), :] = out[:, h * 128:(h + 1) * 128]

    def own_plane(t, carry):
        x, yb = t // 2, lax.rem(t, 2)

        def load(b):
            return v[:, 4 * sg + x, pl.ds(pl.multiple_of(b * 16, 16), 16), :]

        to_channels(load, x + 1, yb)
        return carry

    lax.fori_loop(0, 8, own_plane, 0, unroll=UNROLL[0])
    pl.semaphore_wait(barrier, len(partners))

    c_raw = send(0, v.at[:, 4 * sg + 3], halo, xu)
    c_a1y = send(1, a1.at[pl.ds(1, 4), pl.ds(1024, 16)], a1.at[pl.ds(1, 4), pl.ds(0, 16)], {"gy": yu})
    c_a1c = send(2, a1.at[4, pl.ds(1024, 16)], a1.at[0, pl.ds(0, 16)], {**xu, "gy": yu})

    def conv_high(px, t):
        cols = []
        for h in range(2):
            start = pl.multiple_of(t * 128 + h * 64, 16)
            cols.append(jnp.concatenate([a1[2 * px + k, pl.ds(start, 80), :] for k in range(3)], axis=0))
        out = mm(w1[...], jnp.concatenate(cols, axis=1)) + b1[...]
        acts = (out * sigmoid(out)).astype(BF)
        for h in range(2):
            pre[px, pl.ds(pl.multiple_of(t * 64 + h * 32, 32), 32), :] = out[:, h * 128:(h + 1) * 128]
            start = pl.multiple_of(16 + t * 64 + h * 32, 16)
            act[px + 1, pl.ds(start, 32), :] = acts[:, h * 128:(h + 1) * 128]

    def conv_high_1(t, carry):
        conv_high(1, t)
        return carry

    def conv_high_0(t, carry):
        conv_high(0, t)
        return carry

    lax.fori_loop(1, 8, conv_high_1, 0, unroll=UNROLL[1])
    c_a1y.wait_recv()

    @pl.when(my == 0)
    def _():
        a1[1:5, 0:16, :] = jnp.zeros((4, 16, 128), BF)

    conv_high(1, 0)
    c_ax = send(3, act.at[2, pl.ds(16, 512)], act.at[0, pl.ds(16, 512)], xu)
    c_ac = send(4, act.at[2, pl.ds(512, 16)], act.at[0, pl.ds(0, 16)], {**xu, "gy": yu})
    c_raw.wait_recv()

    @pl.when(first_x)
    def _():
        halo[...] = jnp.zeros_like(halo)

    def halo_plane(yb, carry):
        def load(b):
            return halo[:, pl.ds(pl.multiple_of(b * 16, 16), 16), :]

        to_channels(load, 0, yb)
        return carry

    lax.fori_loop(0, 2, halo_plane, 0, unroll=UNROLL[2])
    c_a1c.wait_recv()

    @pl.when(jnp.logical_or(first_x, my == 0))
    def _():
        a1[0, 0:16, :] = jnp.zeros((16, 128), BF)

    conv_high(0, 7)
    c_ay = send(5, act.at[pl.ds(1, 2), pl.ds(512, 16)], act.at[pl.ds(1, 2), pl.ds(0, 16)], {"gy": yu})
    lax.fori_loop(0, 7, conv_high_0, 0, unroll=UNROLL[1])

    def to_taps(xs, first, count):
        low = act[xs, pl.ds(pl.multiple_of(16 * first, 16), 16 * count), :]
        high = act[xs, pl.ds(pl.multiple_of(256 + 16 * first, 16), 16 * count), :]
        d = mm(jnp.concatenate([low, high], axis=1), s2[...]).astype(BF)
        for t in range(count):
            for k in range(3):
                row = pl.multiple_of(((first + t) * 3 + k) * 16, 16)
                taps[xs, pl.ds(row, 16), :] = d[16 * t:16 * (t + 1), 128 * k:128 * (k + 1)]

    def taps_own(t, carry):
        to_taps(1 + t // 4, 1 + 4 * lax.rem(t, 4), 4)
        return carry

    def taps_halo(t, carry):
        to_taps(0, 1 + 4 * t, 4)
        return carry

    lax.fori_loop(0, 8, taps_own, 0, unroll=UNROLL[3])
    c_ay.wait_recv()
    c_ac.wait_recv()

    @pl.when(my == 0)
    def _():
        act[:, 0:16, :] = jnp.zeros((3, 16, 128), BF)

    to_taps(1, 0, 1)
    to_taps(2, 0, 1)
    c_ax.wait_recv()

    @pl.when(first_x)
    def _():
        act[0] = jnp.zeros((528, 128), BF)

    to_taps(0, 0, 1)
    lax.fori_loop(0, 4, taps_halo, 0, unroll=UNROLL[3])

    def window(j):
        start = pl.multiple_of(j * 96, 16)
        return jnp.concatenate([taps[k, pl.ds(start, 144), :] for k in range(3)], axis=0)

    def conv_low(t, total):
        out = mm(wl[...], jnp.concatenate([window(2 * t), window(2 * t + 1)], axis=1)) + bl[...]
        sig = sigmoid(out)
        slopes = (sig * (1.0 + out * (1.0 - sig))).astype(BF)
        values = out * sig
        for h in range(2):
            slope[0, pl.ds(pl.multiple_of(t * 64 + h * 32, 32), 32), :] = slopes[:, h * 128:(h + 1) * 128]
        return total + values[:, :128] + values[:, 128:]

    total = lax.fori_loop(0, 4, conv_low, jnp.zeros((32, 128), F32), unroll=UNROLL[4])

    lane = lax.broadcasted_iota(jnp.int32, (32, 128), 1)
    row = lax.broadcasted_iota(jnp.int32, (32, 128), 0)
    sums = jnp.sum(total, axis=1, keepdims=True)
    mine = jnp.broadcast_to(jnp.sum(jnp.where(lane == row, sums, 0.0), axis=0, keepdims=True), (8, 128))
    pool_s[0] = mine
    pool_1[mx] = mine
    spread(0, nx, mx, column, pool_1, lambda peer: pool_s.at[0])

    c_sx = send(6, slope.at[0], slope.at[1], xd)
    c_sy = send(7, slope.at[0, pl.ds(0, 32)], slope_y.at[0], {"gy": yd})
    c_sc = send(8, slope.at[0, pl.ds(0, 32)], slope_y.at[1], {**xd, "gy": yd})

    def low_back(t, carry):
        g, gb = carry
        us, ws = [], []
        for h in range(2):
            u = slope[0, pl.ds(pl.multiple_of(t * 64 + h * 32, 32), 32), :]
            us.append(u)
            ws.append(window(2 * t + h))
            gb = gb + u.astype(F32)
        g = g + mm_nt(jnp.concatenate(us, axis=1), jnp.concatenate(ws, axis=1))
        return g, gb

    g_low, gb_low = lax.fori_loop(
        0, 4, low_back, (jnp.zeros((32, 432), F32), jnp.zeros((32, 128), F32)), unroll=UNROLL[5]
    )
    last = jnp.concatenate(
        [g_low[:, 384:432], jnp.sum(gb_low, axis=1, keepdims=True), jnp.zeros((32, 79), F32)], axis=1
    )
    blocks = [g_low[:, 0:128], g_low[:, 128:256], g_low[:, 256:384], last]
    for b in range(4):
        for c in range(4):
            gsend[b * 4 + c] = blocks[c][8 * b:8 * (b + 1), :]
    per = 16 // nx
    g_1[mx] = gsend[pl.ds(mx * per, per)]
    spread(1, nx, mx, column, g_1, lambda peer: gsend.at[pl.ds(peer * per, per)])

    def spread_rows(px, t):
        u = slope[px, pl.ds(pl.multiple_of(t * 32, 32), 32), :]
        d = mm(u, e1[...]).astype(BF)
        for h in range(2):
            for k in range(3):
                start = pl.multiple_of(((8 * h + t) * 3 + k) * 32, 32)
                col = (h * 3 + k) * 128
                up[px, pl.ds(start, 32), :] = d[:, col:col + 128]

    def spread_own(t, carry):
        spread_rows(0, t)
        return carry

    def spread_halo(t, carry):
        spread_rows(1, t)
        return carry

    lax.fori_loop(0, 8, spread_own, 0, unroll=UNROLL[6])

    arrive(0, pool_1, nx)
    part = add_up(pool_1, nx)
    pool_s[1] = part
    pool_2[mg] = part
    spread(2, group, mg, member, pool_2, lambda peer: pool_s.at[1])

    c_sx.wait_recv()
    c_sy.wait_recv()
    c_sc.wait_recv()

    @pl.when(last_x)
    def _():
        slope[1] = jnp.zeros((256, 128), BF)
        slope_y[1] = jnp.zeros((32, 128), BF)

    @pl.when(my == ny - 1)
    def _():
        slope_y[...] = jnp.zeros((2, 32, 128), BF)

    lax.fori_loop(0, 8, spread_halo, 0, unroll=UNROLL[6])
    for px in range(2):
        d = mm(slope_y[px], e1[:, 0:384]).astype(BF)
        for k in range(3):
            up[px, (48 + k) * 32:(49 + k) * 32, :] = d[:, k * 128:(k + 1) * 128]

    def slope_high(t, carry):
        px, yp = t // 8, lax.rem(t, 8)
        at = pl.ds(pl.multiple_of(yp * 64, 64), 64)
        val = pre[px, at, :]
        sig = sigmoid(val)
        pre[px, at, :] = sig * (1.0 + val * (1.0 - sig))
        return carry

    lax.fori_loop(0, 16, slope_high, 0, unroll=UNROLL[7])

    arrive(1, g_1, nx)
    part = add_up(g_1, nx)
    g_2s[...] = part
    g_2[mg] = part
    spread(3, group, mg, member, g_2, lambda peer: g_2s)

    arrive(2, pool_2, group)
    part = add_up(pool_2, group)
    scale = 1.0 / cells
    pooled = jnp.sum(jnp.where(lane == row, part[0:1, :], 0.0), axis=1, keepdims=True) * scale
    weight = hw[...]
    predicted = jnp.sum(pooled * weight, axis=0, keepdims=True) + hb[...]
    error = predicted - tg[...]
    pred_out[...] = predicted
    head_out[...] = pooled * error
    signal = jnp.sum(weight * error, axis=1, keepdims=True)
    lanes = lax.rem(lax.broadcasted_iota(jnp.int32, (32, 384), 1), 32)
    rows = lax.broadcasted_iota(jnp.int32, (32, 384), 0)
    signal_row = jnp.sum(jnp.where(lanes == rows, signal, 0.0), axis=0, keepdims=True)
    weights = (wb[...].astype(F32) * signal_row).astype(BF)

    def high_back(t, carry):
        g, gb = carry
        cols = []
        for h in range(2):
            start = pl.multiple_of(t * 192 + h * 96, 32)
            cols.append(jnp.concatenate([up[0, pl.ds(start, 192), :], up[1, pl.ds(start, 192), :]], axis=0))
        out = mm(weights, jnp.concatenate(cols, axis=1)).astype(BF)
        ws, ups = [], []
        for h in range(2):
            at = pl.ds(pl.multiple_of(t * 64 + h * 32, 32), 32)
            begin = pl.multiple_of(t * 128 + h * 64, 16)
            for qx in range(2):
                tile = out[32 * qx:32 * (qx + 1), h * 128:(h + 1) * 128]
                grad_b[qx, at, :] = tile
                u = (tile.astype(F32) * pre[qx, at, :]).astype(BF)
                gb = gb + u.astype(F32)
                ups.append(u)
                ws.append(jnp.concatenate([a1[2 * qx + k, pl.ds(begin, 80), :] for k in range(3)], axis=0))
        g = g + mm_nt(jnp.concatenate(ups, axis=1), jnp.concatenate(ws, axis=1))
        return g, gb

    g_high, gb_high = lax.fori_loop(
        0, 8, high_back, (jnp.zeros((32, 240), F32), jnp.zeros((32, 128), F32)), unroll=UNROLL[8]
    )
    g_w = select(g_high[0:16], oh[0]) + select(g_high[16:32], oh[1])
    bias = jnp.sum(gb_high, axis=1, keepdims=True)
    lane16 = lax.broadcasted_iota(jnp.int32, (16, 128), 1)
    h_mine = jnp.where(lane16 == 108, bias[0:16] + bias[16:32], g_w) * scale
    h_s[0] = h_mine
    h_1[mx] = h_mine
    spread(4, nx, mx, column, h_1, lambda peer: h_s.at[0])

    arrive(3, g_2, group)
    part = add_up(g_2, group)
    g_3[mx] = part
    spread(5, nx, mx, column, g_3, lambda peer: g_3.at[mx])

    def place(t, carry):
        qx = t // 2
        h = lax.rem(t, 2)
        block = grad_b[qx, pl.ds(pl.multiple_of(h * 256, 256), 256), :]
        out = mm(p2[...], block).astype(BF).reshape(16, 16, 128)
        bg_out[:, 2 * sg + qx, pl.ds(pl.multiple_of(h * 16, 16), 16), :] = out
        return carry

    lax.fori_loop(0, 4, place, 0, unroll=UNROLL[9])
    half = bg_out.at[:, pl.ds(2 * sg, 2)]
    c_bg = send(9, half, half, {"segment": 1 - sg})

    arrive(4, h_1, nx)
    part = add_up(h_1, nx)
    h_s[1] = part
    h_2[mg] = part
    spread(6, group, mg, member, h_2, lambda peer: h_s.at[1])

    arrive(5, g_3, nx)
    bands = []
    for b in range(4):
        bands.append(jnp.concatenate([g_3[(b * 4 + c) // per, (b * 4 + c) % per] for c in range(4)], axis=1))
    g_all = jnp.concatenate(bands, axis=0) * (signal * scale)
    low_out[...] = select(g_all, ol[...])
    low_bias[...] = g_all[:, 432:433]

    arrive(6, h_2, group)
    high_out[...] = add_up(h_2, group)
    c_bg.wait_recv()
    for copy in copies:
        copy.wait_send()
    for stage, buffer, n in stages:
        ref = buffer.at[pl.ds(0, n - 1)]
        pltpu.make_async_copy(ref, ref, ss.at[stage]).wait()


def shards(nx, ny, volume, weight_high, bias_high, weight_low, bias_low, head_weight, head_bias, targets):
    cells = 2 * nx * 16 * ny * 64
    wh = jnp.transpose(weight_high, (0, 2, 3, 4, 1))
    wh = jnp.pad(wh, ((0, 0), (0, 0), (0, 0), (0, 1), (0, 0))).reshape(16, 3, 3, 16)
    w1 = jnp.concatenate(
        [
            jnp.pad(wh, ((0, 0), (0, 0), (0, 2), (0, 0))).reshape(16, 240),
            jnp.pad(wh, ((0, 0), (0, 0), (2, 0), (0, 0))).reshape(16, 240),
        ],
        axis=0,
    )
    wl = jnp.transpose(weight_low, (0, 2, 3, 4, 1)).reshape(32, 432)
    wt = jnp.transpose(weight_low, (1, 2, 3, 4, 0))
    wt = jnp.pad(wt, ((0, 0), (0, 1), (0, 1), (0, 0), (0, 0)))
    tap = ((1, 3), (2, 0))
    wb = jnp.stack(
        [
            jnp.stack([wt[:, tap[sx][dx], tap[sy][dy]] for dx in range(2) for dy in range(2)], axis=1)
            for sx in range(2)
            for sy in range(2)
        ],
        axis=0,
    ).reshape(64, 384)
    b1 = jnp.concatenate([bias_high, bias_high])[:, None]
    makers = (depth_taps, rows_to_channels, depth_taps_low, depth_spread, channels_to_rows, low_order, high_order)
    tables = [jnp.asarray(t().astype(np.float32), BF) for t in makers]
    vm = pl.BlockSpec(memory_space=pltpu.VMEM)
    dma = pltpu.SemaphoreType.DMA
    per = 16 // nx
    group = 2 * ny
    bg, pred, head, low, low_bias, high = pl.pallas_call(
        functools.partial(kernel, nx, ny, cells),
        out_shape=(
            jax.ShapeDtypeStruct((16, 4, 32, 128), BF),
            jax.ShapeDtypeStruct((1, 4), F32),
            jax.ShapeDtypeStruct((32, 4), F32),
            jax.ShapeDtypeStruct((32, 432), F32),
            jax.ShapeDtypeStruct((32, 1), F32),
            jax.ShapeDtypeStruct((16, 128), F32),
        ),
        in_specs=[vm] * 16,
        out_specs=(vm,) * 6,
        scratch_shapes=[
            pltpu.VMEM((4, 64, 256), BF),
            pltpu.VMEM((5, 1040, 128), BF),
            pltpu.VMEM((2, 512, 128), F32),
            pltpu.VMEM((3, 528, 128), BF),
            pltpu.VMEM((3, 816, 128), BF),
            pltpu.VMEM((2, 256, 128), BF),
            pltpu.VMEM((2, 32, 128), BF),
            pltpu.VMEM((2, 1632, 128), BF),
            pltpu.VMEM((2, 512, 128), BF),
            pltpu.VMEM((2, 8, 128), F32),
            pltpu.VMEM((nx, 8, 128), F32),
            pltpu.VMEM((group, 8, 128), F32),
            pltpu.VMEM((16, 8, 128), F32),
            pltpu.VMEM((nx, per, 8, 128), F32),
            pltpu.VMEM((per, 8, 128), F32),
            pltpu.VMEM((group, per, 8, 128), F32),
            pltpu.VMEM((nx, per, 8, 128), F32),
            pltpu.VMEM((2, 16, 128), F32),
            pltpu.VMEM((nx, 16, 128), F32),
            pltpu.VMEM((group, 16, 128), F32),
            dma((10,)), dma((10,)), dma((7,)), dma((7,)),
        ],
        compiler_params=pltpu.CompilerParams(
            collective_id=0, has_side_effects=True, vmem_limit_bytes=48 << 20
        ),
        name="fused",
    )(
        volume, w1, b1, wl, bias_low[:, None], head_weight, head_bias[None], targets[None], wb, *tables
    )
    return (
        pred[0],
        bg,
        high[:, :108].reshape(16, 4, 3, 3, 3),
        high[:, 108],
        low.reshape(32, 16, 3, 3, 3),
        low_bias[:, 0],
        head,
    )


def solution(mesh):
    nx, ny = mesh.shape["gx"], mesh.shape["gy"]
    placed = (P(None, "gx", "gy", None), P(), P(), P(), P(), P(), P(), P())
    return jax.shard_map(
        functools.partial(shards, nx, ny),
        mesh=mesh,
        in_specs=placed,
        out_specs=(P(), P(None, "gx", "gy", None), P(), P(), P(), P(), P()),
        check_vma=False,
    )
```

```python
import functools

import jax
import jax.numpy as jnp
import numpy as np
from jax import lax
from jax.experimental import pallas as pl
from jax.experimental.pallas import tpu as pltpu
from jax.sharding import PartitionSpec as P

MESH = pl.DeviceIdType.MESH
BF = jnp.bfloat16
F32 = jnp.float32
UNROLL = (8, 4, 2, 4, 4, 4, 4, 4, 8, 4)


def depth_taps():
    z = np.arange(256)[:, None, None]
    k = np.arange(3)[None, :, None]
    p = np.arange(128)[None, None, :]
    return (z == 2 * p + k - 1).reshape(256, 384)


def rows_to_channels():
    out = np.zeros((16, 16, 12, 16), bool)
    for r in range(12):
        for y in range(16):
            out[y, r, r, y] = True
    return out.reshape(256, 192)


def depth_taps_low():
    out = np.zeros((2, 128, 3, 2, 64), bool)
    for h in range(2):
        for k in range(3):
            for p in range(64):
                if 2 * p + k - 1 >= 0:
                    out[h, 2 * p + k - 1, k, h, p] = True
    return out.reshape(256, 384)


def depth_spread():
    out = np.zeros((2, 64, 2, 3, 128), bool)
    for h in range(2):
        for k in range(3):
            for p in range(64):
                if 2 * p + k - 1 >= 0:
                    out[h, p, h, k, 2 * p + k - 1] = True
    return out.reshape(128, 768)


def channels_to_rows():
    out = np.zeros((16, 16, 16, 16), bool)
    for i in range(16):
        for y in range(16):
            out[i, y, y, i] = True
    return out.reshape(256, 256)


def high_order():
    out = np.zeros((2, 3, 5, 16, 128), bool)
    for s in range(2):
        for kx in range(3):
            for ky in range(3):
                for kz in range(3):
                    for c in range(4):
                        out[s, kx, ky + 2 * s, kz * 4 + c, ((kx * 3 + ky) * 3 + kz) * 4 + c] = True
    return out.reshape(2, 240, 128)


def early_tables():
    out = np.zeros((256, 896), np.float32)
    out[:, 0:384] = depth_taps()
    out[:, 384:576] = rows_to_channels()
    out[0:240, 640:768], out[0:240, 768:896] = high_order()
    return out


def late_tables():
    out = np.zeros((256, 1024), np.float32)
    out[:, 0:384] = depth_taps_low()
    out[:, 384:640] = channels_to_rows()
    spread = depth_spread()
    out[0:128, 640:1024] = spread[:, 0:384]
    out[128:256, 640:1024] = spread[:, 384:768]
    return out


def mm(a, b):
    return lax.dot_general(a, b, (((1,), (0,)), ((), ())), preferred_element_type=F32)


def mm_nt(a, b):
    return lax.dot_general(a, b, (((1,), (1,)), ((), ())), preferred_element_type=F32)


def thirds(x):
    a = x.astype(BF)
    rest = x - a.astype(F32)
    b = rest.astype(BF)
    c = (rest - b.astype(F32)).astype(BF)
    return jnp.concatenate([a, b, c], axis=0)


def select(x, table):
    n = x.shape[0]
    out = mm(thirds(x), table)
    return out[0:n] + out[n:2 * n] + out[2 * n:3 * n]


def sigmoid(x):
    return jax.nn.sigmoid(x)


def kernel(
    nx, ny, cells,
    v_hbm, ta_hbm, tb_hbm, *rest,
):
    small_hbm, rest = rest[:7], rest[7:]
    (
        bg_out, pred_out, head_out, low_out, low_bias, high_out, high_bias,
        v, ta, tb, wh, wlt, bh_row, bl_row, hw, hb_row, tg_row,
        w_tall, wl, wb, h_tall, ls,
        halo, a1, pre, act, taps, slope, slope_y, up, grad_b,
        pool_s, pool_1, pool_2, gsend, g_1, g_2s, g_2, g_3, h_s, h_1, h_2,
        hs, hr, ss, rs,
    ) = rest
    sg = lax.axis_index("segment")
    mx = lax.axis_index("gx")
    my = lax.axis_index("gy")
    group = 2 * ny
    mg = sg * ny + my
    yu, yd = lax.rem(my + 1, ny), lax.rem(my + ny - 1, ny)
    xu = {"segment": 1 - sg, "gx": lax.rem(mx + sg, nx)}
    xd = {"segment": 1 - sg, "gx": lax.rem(mx + nx - 1 + sg, nx)}
    first_x = jnp.logical_and(mx == 0, sg == 0)
    last_x = jnp.logical_and(mx == nx - 1, sg == 1)

    loads = [
        pltpu.make_async_copy(v_hbm.at[:, pl.ds(4 * sg, 4)], v, ls.at[0]),
        pltpu.make_async_copy(ta_hbm, ta, ls.at[1]),
    ]
    for n, (src, dst) in enumerate(zip(small_hbm, (wh, wlt, bh_row, bl_row, hw, hb_row, tg_row))):
        loads.append(pltpu.make_async_copy(src, dst, ls.at[2 + n]))
    loads.append(pltpu.make_async_copy(tb_hbm, tb, ls.at[9]))
    for load in loads:
        load.start()

    columns, members = [], []
    if nx == 16:
        far = [(a, b) for a in range(4) for b in range(4) if a or b]
        far.sort(key=lambda t: -min(t[0], 4 - t[0]) - min(t[1], 4 - t[1]))
        for a, b in far:
            at = lax.rem(mx // 4 + a, 4) * 4 + lax.rem(lax.rem(mx, 4) + b, 4)
            columns.append((at, {"gx": at}))
    else:
        for d in range(1, nx):
            at = lax.rem(mx + d, nx)
            columns.append((at, {"gx": at}))
    far = [(a, b) for a in range(2) for b in range(ny) if a or b]
    far.sort(key=lambda t: -min(t[1], ny - t[1]))
    for a, b in far:
        seg = 1 - sg if a else sg
        at = lax.rem(my + b, ny)
        members.append((seg * ny + at, {"segment": seg, "gy": at}))

    barrier = pltpu.get_barrier_semaphore()
    partners = [peer for _, peer in columns + members]
    partners += [xu, xd, {**xu, "gy": yu}, {**xd, "gy": yd}]
    for peer in partners:
        pl.semaphore_signal(barrier, inc=1, device_id=peer, device_id_type=MESH)

    copies = []

    def send(n, src, dst, peer):
        copy = pltpu.make_async_remote_copy(
            src_ref=src, dst_ref=dst, send_sem=hs.at[n], recv_sem=hr.at[n],
            device_id=peer, device_id_type=MESH,
        )
        copy.start()
        copies.append(copy)
        return copy

    stages = []

    def spread(stage, me, peers, buffer, source):
        for at, peer in peers:
            pltpu.make_async_remote_copy(
                src_ref=source(at), dst_ref=buffer.at[me],
                send_sem=ss.at[stage], recv_sem=rs.at[stage],
                device_id=peer, device_id_type=MESH,
            ).start()
        stages.append((stage, buffer, len(peers) + 1))

    def arrive(stage, buffer, n):
        ref = buffer.at[pl.ds(0, n - 1)]
        pltpu.make_async_copy(ref, ref, rs.at[stage]).wait()

    def add_up(buffer, n):
        part = buffer[0]
        for d in range(1, n):
            part = part + buffer[d]
        return part

    def to_channels(load, xs, yb):
        parts = []
        for h in range(2):
            raw = load(yb * 2 + h).reshape(64, 256)
            d = mm(raw, ta[:, 0:384]).astype(BF)
            parts.append(jnp.concatenate([d[:, 0:128], d[:, 128:256], d[:, 256:384]], axis=0))
        out = mm(ta[:, 384:576], jnp.concatenate(parts, axis=1)).astype(BF)
        for h in range(2):
            start = pl.multiple_of(16 + (yb * 2 + h) * 256, 16)
            a1[xs, pl.ds(start, 256), :] = out[:, h * 128:(h + 1) * 128]

    def own_plane(t, carry):
        x, yb = t // 2, lax.rem(t, 2)

        def load(b):
            return v[:, x, pl.ds(pl.multiple_of(b * 16, 16), 16), :]

        to_channels(load, x + 1, yb)
        return carry

    loads[0].wait()
    loads[1].wait()
    lax.fori_loop(0, 8, own_plane, 0, unroll=UNROLL[0])

    for load in loads[2:]:
        load.wait()

    def eye(n):
        r = lax.broadcasted_iota(jnp.int32, (n, n), 0)
        return r == lax.broadcasted_iota(jnp.int32, (n, n), 1)

    def to_column(row):
        n = row.shape[1]
        return jnp.sum(jnp.where(eye(n), row, 0.0), axis=1, keepdims=True)

    w_tall[...] = jnp.zeros_like(w_tall)
    for t in range(27):
        w_tall[4 * t:4 * t + 4, :] = wh[t].astype(F32)
    w_flat = mm_nt(eye(16).astype(F32).astype(BF), w_tall[...].astype(BF)).astype(BF)
    w1 = jnp.concatenate(
        [mm_nt(w_flat, ta[0:240, 640:768]), mm_nt(w_flat, ta[0:240, 768:896])], axis=0
    ).astype(BF)
    wl[...] = mm_nt(eye(32).astype(F32).astype(BF), wlt[...]).astype(BF)
    b1 = to_column(bh_row[...])
    b1 = jnp.concatenate([b1, b1], axis=0)
    bl = to_column(bl_row[...])

    pl.semaphore_wait(barrier, len(partners))

    c_raw = send(0, v.at[:, 3], halo, xu)
    c_a1y = send(1, a1.at[pl.ds(1, 4), pl.ds(1024, 16)], a1.at[pl.ds(1, 4), pl.ds(0, 16)], {"gy": yu})
    c_a1c = send(2, a1.at[4, pl.ds(1024, 16)], a1.at[0, pl.ds(0, 16)], {**xu, "gy": yu})

    def conv_high(px, t):
        cols = []
        for h in range(2):
            start = pl.multiple_of(t * 128 + h * 64, 16)
            cols.append(jnp.concatenate([a1[2 * px + k, pl.ds(start, 80), :] for k in range(3)], axis=0))
        out = mm(w1, jnp.concatenate(cols, axis=1)) + b1
        acts = (out * sigmoid(out)).astype(BF)
        for h in range(2):
            pre[px, pl.ds(pl.multiple_of(t * 64 + h * 32, 32), 32), :] = out[:, h * 128:(h + 1) * 128]
            start = pl.multiple_of(16 + t * 64 + h * 32, 16)
            act[px + 1, pl.ds(start, 32), :] = acts[:, h * 128:(h + 1) * 128]

    def conv_high_1(t, carry):
        conv_high(1, t)
        return carry

    def conv_high_0(t, carry):
        conv_high(0, t)
        return carry

    lax.fori_loop(1, 8, conv_high_1, 0, unroll=UNROLL[1])
    c_a1y.wait_recv()

    @pl.when(my == 0)
    def _():
        a1[1:5, 0:16, :] = jnp.zeros((4, 16, 128), BF)

    conv_high(1, 0)
    c_ax = send(3, act.at[2, pl.ds(16, 512)], act.at[0, pl.ds(16, 512)], xu)
    c_ac = send(4, act.at[2, pl.ds(512, 16)], act.at[0, pl.ds(0, 16)], {**xu, "gy": yu})
    c_raw.wait_recv()

    @pl.when(first_x)
    def _():
        halo[...] = jnp.zeros_like(halo)

    def halo_plane(yb, carry):
        def load(b):
            return halo[:, pl.ds(pl.multiple_of(b * 16, 16), 16), :]

        to_channels(load, 0, yb)
        return carry

    lax.fori_loop(0, 2, halo_plane, 0, unroll=UNROLL[2])
    c_a1c.wait_recv()

    @pl.when(jnp.logical_or(first_x, my == 0))
    def _():
        a1[0, 0:16, :] = jnp.zeros((16, 128), BF)

    conv_high(0, 7)
    c_ay = send(5, act.at[pl.ds(1, 2), pl.ds(512, 16)], act.at[pl.ds(1, 2), pl.ds(0, 16)], {"gy": yu})
    lax.fori_loop(0, 7, conv_high_0, 0, unroll=UNROLL[1])

    def to_taps(xs, first, count):
        low = act[xs, pl.ds(pl.multiple_of(16 * first, 16), 16 * count), :]
        high = act[xs, pl.ds(pl.multiple_of(256 + 16 * first, 16), 16 * count), :]
        d = mm(jnp.concatenate([low, high], axis=1), tb[:, 0:384]).astype(BF)
        for t in range(count):
            for k in range(3):
                row = pl.multiple_of(((first + t) * 3 + k) * 16, 16)
                taps[xs, pl.ds(row, 16), :] = d[16 * t:16 * (t + 1), 128 * k:128 * (k + 1)]

    def taps_own(t, carry):
        to_taps(1 + t // 4, 1 + 4 * lax.rem(t, 4), 4)
        return carry

    def taps_halo(t, carry):
        to_taps(0, 1 + 4 * t, 4)
        return carry

    lax.fori_loop(0, 8, taps_own, 0, unroll=UNROLL[3])
    c_ay.wait_recv()
    c_ac.wait_recv()

    @pl.when(my == 0)
    def _():
        act[:, 0:16, :] = jnp.zeros((3, 16, 128), BF)

    to_taps(1, 0, 1)
    to_taps(2, 0, 1)
    c_ax.wait_recv()

    @pl.when(first_x)
    def _():
        act[0] = jnp.zeros((528, 128), BF)

    to_taps(0, 0, 1)
    lax.fori_loop(0, 4, taps_halo, 0, unroll=UNROLL[3])

    def window(j):
        start = pl.multiple_of(j * 96, 16)
        return jnp.concatenate([taps[k, pl.ds(start, 144), :] for k in range(3)], axis=0)

    def conv_low(t, total):
        out = mm(wl[...], jnp.concatenate([window(2 * t), window(2 * t + 1)], axis=1)) + bl
        sig = sigmoid(out)
        slopes = (sig * (1.0 + out * (1.0 - sig))).astype(BF)
        values = out * sig
        for h in range(2):
            slope[0, pl.ds(pl.multiple_of(t * 64 + h * 32, 32), 32), :] = slopes[:, h * 128:(h + 1) * 128]
        return total + values[:, :128] + values[:, 128:]

    total = lax.fori_loop(0, 4, conv_low, jnp.zeros((32, 128), F32), unroll=UNROLL[4])

    lane = lax.broadcasted_iota(jnp.int32, (32, 128), 1)
    row = lax.broadcasted_iota(jnp.int32, (32, 128), 0)
    sums = jnp.sum(total, axis=1, keepdims=True)
    mine = jnp.broadcast_to(jnp.sum(jnp.where(lane == row, sums, 0.0), axis=0, keepdims=True), (8, 128))
    pool_s[0] = mine
    pool_1[mx] = mine
    spread(0, mx, columns, pool_1, lambda peer: pool_s.at[0])

    c_sx = send(6, slope.at[0], slope.at[1], xd)
    c_sy = send(7, slope.at[0, pl.ds(0, 32)], slope_y.at[0], {"gy": yd})
    c_sc = send(8, slope.at[0, pl.ds(0, 32)], slope_y.at[1], {**xd, "gy": yd})

    def low_back(t, carry):
        g, gb = carry
        us, ws = [], []
        for h in range(2):
            u = slope[0, pl.ds(pl.multiple_of(t * 64 + h * 32, 32), 32), :]
            us.append(u)
            ws.append(window(2 * t + h))
            gb = gb + u.astype(F32)
        g = g + mm_nt(jnp.concatenate(us, axis=1), jnp.concatenate(ws, axis=1))
        return g, gb

    g_low, gb_low = lax.fori_loop(
        0, 4, low_back, (jnp.zeros((32, 432), F32), jnp.zeros((32, 128), F32)), unroll=UNROLL[5]
    )
    last = jnp.concatenate(
        [g_low[:, 384:432], jnp.sum(gb_low, axis=1, keepdims=True), jnp.zeros((32, 79), F32)], axis=1
    )
    blocks = [g_low[:, 0:128], g_low[:, 128:256], g_low[:, 256:384], last]
    for b in range(4):
        for c in range(4):
            gsend[b * 4 + c] = blocks[c][8 * b:8 * (b + 1), :]
    per = 16 // nx
    g_1[mx] = gsend[pl.ds(mx * per, per)]
    spread(1, mx, columns, g_1, lambda peer: gsend.at[pl.ds(peer * per, per)])

    def spread_rows(px, t):
        u = slope[px, pl.ds(pl.multiple_of(t * 32, 32), 32), :]
        for h in range(2):
            d = mm(u, tb[128 * h:128 * (h + 1), 640:1024]).astype(BF)
            for k in range(3):
                start = pl.multiple_of(((8 * h + t) * 3 + k) * 32, 32)
                up[px, pl.ds(start, 32), :] = d[:, k * 128:(k + 1) * 128]

    def spread_own(t, carry):
        spread_rows(0, t)
        return carry

    def spread_halo(t, carry):
        spread_rows(1, t)
        return carry

    lax.fori_loop(0, 8, spread_own, 0, unroll=UNROLL[6])

    arrive(0, pool_1, nx)
    part = add_up(pool_1, nx)
    pool_s[1] = part
    pool_2[mg] = part
    spread(2, mg, members, pool_2, lambda peer: pool_s.at[1])

    c_sx.wait_recv()
    c_sy.wait_recv()
    c_sc.wait_recv()

    @pl.when(last_x)
    def _():
        slope[1] = jnp.zeros((256, 128), BF)
        slope_y[1] = jnp.zeros((32, 128), BF)

    @pl.when(my == ny - 1)
    def _():
        slope_y[...] = jnp.zeros((2, 32, 128), BF)

    lax.fori_loop(0, 8, spread_halo, 0, unroll=UNROLL[6])
    for px in range(2):
        d = mm(slope_y[px], tb[0:128, 640:1024]).astype(BF)
        for k in range(3):
            up[px, (48 + k) * 32:(49 + k) * 32, :] = d[:, k * 128:(k + 1) * 128]

    def slope_high(t, carry):
        px, yp = t // 8, lax.rem(t, 8)
        at = pl.ds(pl.multiple_of(yp * 64, 64), 64)
        val = pre[px, at, :]
        sig = sigmoid(val)
        pre[px, at, :] = sig * (1.0 + val * (1.0 - sig))
        return carry

    lax.fori_loop(0, 16, slope_high, 0, unroll=UNROLL[7])

    wb[...] = jnp.zeros_like(wb)
    for kx in range(3):
        for ky in range(3):
            for kz in range(3):
                r = (2 * (kx != 1) + (ky != 1)) * 16
                c = (2 * (kx == 0) + (ky == 0)) * 96 + kz * 32
                t = ((kx * 3 + ky) * 3 + kz) * 16
                wb[r:r + 16, c:c + 32] = wlt[t:t + 16, :]

    arrive(1, g_1, nx)
    part = add_up(g_1, nx)
    g_2s[...] = part
    g_2[mg] = part
    spread(3, mg, members, g_2, lambda peer: g_2s)

    arrive(2, pool_2, group)
    part = add_up(pool_2, group)
    scale = 1.0 / cells
    pooled = part[0:1, 0:32] * scale
    weight = hw[...]
    predicted = jnp.sum(weight * pooled, axis=1, keepdims=True) + to_column(hb_row[...])
    error = predicted - to_column(tg_row[...])
    signal = jnp.sum(weight * error, axis=0, keepdims=True)
    weights = (wb[...].astype(F32) * jnp.concatenate([signal] * 12, axis=1)).astype(BF)

    def high_back(t, carry):
        g, gb = carry
        cols = []
        for h in range(2):
            start = pl.multiple_of(t * 192 + h * 96, 32)
            cols.append(jnp.concatenate([up[0, pl.ds(start, 192), :], up[1, pl.ds(start, 192), :]], axis=0))
        out = mm(weights, jnp.concatenate(cols, axis=1)).astype(BF)
        ws, ups = [], []
        for h in range(2):
            at = pl.ds(pl.multiple_of(t * 64 + h * 32, 32), 32)
            begin = pl.multiple_of(t * 128 + h * 64, 16)
            for qx in range(2):
                tile = out[32 * qx:32 * (qx + 1), h * 128:(h + 1) * 128]
                grad_b[qx, at, :] = tile
                u = (tile.astype(F32) * pre[qx, at, :]).astype(BF)
                gb = gb + u.astype(F32)
                ups.append(u)
                ws.append(jnp.concatenate([a1[2 * qx + k, pl.ds(begin, 80), :] for k in range(3)], axis=0))
        g = g + mm_nt(jnp.concatenate(ups, axis=1), jnp.concatenate(ws, axis=1))
        return g, gb

    g_high, gb_high = lax.fori_loop(
        0, 8, high_back, (jnp.zeros((32, 240), F32), jnp.zeros((32, 128), F32)), unroll=UNROLL[8]
    )
    g_w = select(g_high[0:16], ta[0:240, 640:768]) + select(g_high[16:32], ta[0:240, 768:896])
    bias = jnp.sum(gb_high, axis=1, keepdims=True)
    lane16 = lax.broadcasted_iota(jnp.int32, (16, 128), 1)
    h_mine = jnp.where(lane16 == 108, bias[0:16] + bias[16:32], g_w) * scale
    h_s[0] = h_mine
    h_1[mx] = h_mine
    spread(4, mx, columns, h_1, lambda peer: h_s.at[0])

    arrive(3, g_2, group)
    part = add_up(g_2, group)
    g_3[mx] = part
    spread(5, mx, columns, g_3, lambda peer: g_3.at[mx])

    def place(t, carry):
        qx = t // 2
        h = lax.rem(t, 2)
        block = grad_b[qx, pl.ds(pl.multiple_of(h * 256, 256), 256), :]
        out = mm(tb[:, 384:640], block).astype(BF).reshape(16, 16, 128)
        bg_out[:, 2 * sg + qx, pl.ds(pl.multiple_of(h * 16, 16), 16), :] = out
        return carry

    lax.fori_loop(0, 4, place, 0, unroll=UNROLL[9])
    half = bg_out.at[:, pl.ds(2 * sg, 2)]
    c_bg = send(9, half, half, {"segment": 1 - sg})

    arrive(4, h_1, nx)
    part = add_up(h_1, nx)
    h_s[1] = part
    h_2[mg] = part
    spread(6, mg, members, h_2, lambda peer: h_s.at[1])

    arrive(5, g_3, nx)
    bands = []
    for b in range(4):
        bands.append(jnp.concatenate([g_3[(b * 4 + c) // per, (b * 4 + c) % per] for c in range(4)], axis=1))
    g_all = jnp.transpose(jnp.concatenate(bands, axis=0)) * (signal * scale)
    low_out[...] = g_all[0:432, :]
    low_bias[...] = g_all[432:433, :]
    head_out[...] = error * pooled
    pred_out[...] = jnp.sum(jnp.where(eye(4), predicted, 0.0), axis=0, keepdims=True)

    arrive(6, h_2, group)
    h_tall[...] = jnp.transpose(add_up(h_2, group))
    for t in range(27):
        high_out[t] = h_tall[4 * t:4 * t + 4, :]
    high_bias[...] = h_tall[108:109, :]
    c_bg.wait_recv()
    for copy in copies:
        copy.wait_send()
    for stage, buffer, n in stages:
        ref = buffer.at[pl.ds(0, n - 1)]
        pltpu.make_async_copy(ref, ref, ss.at[stage]).wait()


def finish(*refs):
    sources, results, sem = refs[:7], refs[7:14], refs[14]
    moves = [pltpu.make_async_copy(a, b, sem.at[n]) for n, (a, b) in enumerate(zip(sources, results))]
    for move in moves:
        move.start()
    for move in moves:
        move.wait()


def shards(nx, ny, volume, weight_high, bias_high, weight_low, bias_low, head_weight, head_bias, targets):
    cells = 2 * nx * 16 * ny * 64
    small = (
        jnp.transpose(weight_high, (2, 3, 4, 1, 0)).reshape(27, 4, 16),
        jnp.transpose(weight_low, (2, 3, 4, 1, 0)).reshape(432, 32),
        bias_high[None],
        bias_low[None],
        head_weight.T,
        head_bias[None],
        targets[None],
    )
    tables = [jnp.asarray(t(), BF) for t in (early_tables, late_tables)]
    vm = pl.BlockSpec(memory_space=pltpu.VMEM)
    hbm = pl.BlockSpec(memory_space=pltpu.HBM)
    dma = pltpu.SemaphoreType.DMA
    per = 16 // nx
    group = 2 * ny
    results = (
        jax.ShapeDtypeStruct((16, 4, 32, 128), BF),
        jax.ShapeDtypeStruct((1, 4), F32),
        jax.ShapeDtypeStruct((4, 32), F32),
        jax.ShapeDtypeStruct((432, 32), F32),
        jax.ShapeDtypeStruct((1, 32), F32),
        jax.ShapeDtypeStruct((27, 4, 16), F32),
        jax.ShapeDtypeStruct((1, 16), F32),
    )
    outs = pl.pallas_call(
        functools.partial(kernel, nx, ny, cells),
        out_shape=results,
        in_specs=[hbm] * 10,
        out_specs=(vm,) * 7,
        scratch_shapes=[
            pltpu.VMEM((4, 4, 64, 256), BF),
            pltpu.VMEM((256, 896), BF),
            pltpu.VMEM((256, 1024), BF),
            *(pltpu.VMEM(a.shape, a.dtype) for a in small),
            pltpu.VMEM((128, 16), F32),
            pltpu.VMEM((32, 432), BF),
            pltpu.VMEM((64, 384), BF),
            pltpu.VMEM((128, 16), F32),
            dma((10,)),
            pltpu.VMEM((4, 64, 256), BF),
            pltpu.VMEM((5, 1040, 128), BF),
            pltpu.VMEM((2, 512, 128), F32),
            pltpu.VMEM((3, 528, 128), BF),
            pltpu.VMEM((3, 816, 128), BF),
            pltpu.VMEM((2, 256, 128), BF),
            pltpu.VMEM((2, 32, 128), BF),
            pltpu.VMEM((2, 1632, 128), BF),
            pltpu.VMEM((2, 512, 128), BF),
            pltpu.VMEM((2, 8, 128), F32),
            pltpu.VMEM((nx, 8, 128), F32),
            pltpu.VMEM((group, 8, 128), F32),
            pltpu.VMEM((16, 8, 128), F32),
            pltpu.VMEM((nx, per, 8, 128), F32),
            pltpu.VMEM((per, 8, 128), F32),
            pltpu.VMEM((group, per, 8, 128), F32),
            pltpu.VMEM((nx, per, 8, 128), F32),
            pltpu.VMEM((2, 16, 128), F32),
            pltpu.VMEM((nx, 16, 128), F32),
            pltpu.VMEM((group, 16, 128), F32),
            dma((10,)), dma((10,)), dma((7,)), dma((7,)),
        ],
        compiler_params=pltpu.CompilerParams(
            collective_id=0, has_side_effects=True, vmem_limit_bytes=48 << 20
        ),
        name="fused",
    )(volume, *tables, *small)
    bg, pred, head, low, low_bias, high, high_bias = pl.pallas_call(
        finish,
        out_shape=results,
        in_specs=[vm] * 7,
        out_specs=(hbm,) * 7,
        scratch_shapes=[dma((7,))],
        name="finish",
    )(*outs)
    return (
        pred[0],
        bg,
        jnp.transpose(high.reshape(3, 3, 3, 4, 16), (4, 3, 0, 1, 2)),
        high_bias[0],
        jnp.transpose(low.reshape(3, 3, 3, 16, 32), (4, 3, 0, 1, 2)),
        low_bias[0],
        head.T,
    )


def solution(mesh):
    nx, ny = mesh.shape["gx"], mesh.shape["gy"]
    placed = (P(None, "gx", "gy", None), P(), P(), P(), P(), P(), P(), P())
    return jax.shard_map(
        functools.partial(shards, nx, ny),
        mesh=mesh,
        in_specs=placed,
        out_specs=(P(), P(None, "gx", "gy", None), P(), P(), P(), P(), P()),
        check_vma=False,
    )
```

```python
import functools

import jax
import jax.numpy as jnp
import numpy as np
from jax import lax
from jax.experimental import pallas as pl
from jax.experimental.pallas import tpu as pltpu
from jax.sharding import PartitionSpec as P

MESH = pl.DeviceIdType.MESH
BF = jnp.bfloat16
F32 = jnp.float32
UNROLL = (8, 4, 2, 4, 4, 4, 4, 4, 8, 4)


def depth_taps():
    z = np.arange(256)[:, None, None]
    k = np.arange(3)[None, :, None]
    p = np.arange(128)[None, None, :]
    return (z == 2 * p + k - 1).reshape(256, 384)


def rows_to_channels():
    out = np.zeros((16, 16, 12, 16), bool)
    for r in range(12):
        for y in range(16):
            out[y, r, r, y] = True
    return out.reshape(256, 192)


def depth_taps_low():
    out = np.zeros((2, 128, 3, 2, 64), bool)
    for h in range(2):
        for k in range(3):
            for p in range(64):
                if 2 * p + k - 1 >= 0:
                    out[h, 2 * p + k - 1, k, h, p] = True
    return out.reshape(256, 384)


def depth_spread():
    out = np.zeros((2, 64, 2, 3, 128), bool)
    for h in range(2):
        for k in range(3):
            for p in range(64):
                if 2 * p + k - 1 >= 0:
                    out[h, p, h, k, 2 * p + k - 1] = True
    return out.reshape(128, 768)


def channels_to_rows():
    out = np.zeros((16, 16, 16, 16), bool)
    for i in range(16):
        for y in range(16):
            out[i, y, y, i] = True
    return out.reshape(256, 256)


def high_order():
    out = np.zeros((2, 3, 5, 16, 128), bool)
    for s in range(2):
        for kx in range(3):
            for ky in range(3):
                for kz in range(3):
                    for c in range(4):
                        out[s, kx, ky + 2 * s, kz * 4 + c, ((kx * 3 + ky) * 3 + kz) * 4 + c] = True
    return out.reshape(2, 240, 128)


def early_tables():
    out = np.zeros((256, 896), np.float32)
    out[:, 0:384] = depth_taps()
    out[:, 384:576] = rows_to_channels()
    out[0:240, 640:768], out[0:240, 768:896] = high_order()
    return out


def late_tables():
    out = np.zeros((256, 1024), np.float32)
    out[:, 0:384] = depth_taps_low()
    out[:, 384:640] = channels_to_rows()
    spread = depth_spread()
    out[0:128, 640:1024] = spread[:, 0:384]
    out[128:256, 640:1024] = spread[:, 384:768]
    return out


def mm(a, b):
    return lax.dot_general(a, b, (((1,), (0,)), ((), ())), preferred_element_type=F32)


def mm_nt(a, b):
    return lax.dot_general(a, b, (((1,), (1,)), ((), ())), preferred_element_type=F32)


def thirds(x):
    a = x.astype(BF)
    rest = x - a.astype(F32)
    b = rest.astype(BF)
    c = (rest - b.astype(F32)).astype(BF)
    return jnp.concatenate([a, b, c], axis=0)


def select(x, table):
    n = x.shape[0]
    out = mm(thirds(x), table)
    return out[0:n] + out[n:2 * n] + out[2 * n:3 * n]


def sigmoid(x):
    return jax.nn.sigmoid(x)


def kernel(
    nx, ny, cells,
    v_hbm, ta_hbm, tb_hbm, *rest,
):
    small_hbm, results, rest = rest[:7], rest[7:14], rest[14:]
    (
        bg_out, pred_out, head_out, low_out, low_bias, high_out, high_bias,
        v, ta, tb, wh, wlt, bh_row, bl_row, hw, hb_row, tg_row,
        w_tall, wl, wb, h_tall, ls, os,
        halo, a1, pre, act, taps, slope, slope_y, up, grad_b,
        pool_s, pool_1, pool_2, gsend, g_1, g_2s, g_2, g_3, h_s, h_1, h_2,
        hs, hr, ss, rs,
    ) = rest
    sg = lax.axis_index("segment")
    mx = lax.axis_index("gx")
    my = lax.axis_index("gy")
    group = 2 * ny
    mg = sg * ny + my
    yu, yd = lax.rem(my + 1, ny), lax.rem(my + ny - 1, ny)
    xu = {"segment": 1 - sg, "gx": lax.rem(mx + sg, nx)}
    xd = {"segment": 1 - sg, "gx": lax.rem(mx + nx - 1 + sg, nx)}
    first_x = jnp.logical_and(mx == 0, sg == 0)
    last_x = jnp.logical_and(mx == nx - 1, sg == 1)

    loads = [
        pltpu.make_async_copy(v_hbm.at[:, pl.ds(4 * sg, 4)], v, ls.at[0]),
        pltpu.make_async_copy(ta_hbm, ta, ls.at[1]),
    ]
    for n, (src, dst) in enumerate(zip(small_hbm, (wh, wlt, bh_row, bl_row, hw, hb_row, tg_row))):
        loads.append(pltpu.make_async_copy(src, dst, ls.at[2 + n]))
    loads.append(pltpu.make_async_copy(tb_hbm, tb, ls.at[9]))
    for load in loads:
        load.start()

    columns, members = [], []
    if nx == 16:
        far = [(a, b) for a in range(4) for b in range(4) if a or b]
        far.sort(key=lambda t: -min(t[0], 4 - t[0]) - min(t[1], 4 - t[1]))
        for a, b in far:
            at = lax.rem(mx // 4 + a, 4) * 4 + lax.rem(lax.rem(mx, 4) + b, 4)
            columns.append((at, {"gx": at}))
    else:
        for d in range(1, nx):
            at = lax.rem(mx + d, nx)
            columns.append((at, {"gx": at}))
    far = [(a, b) for a in range(2) for b in range(ny) if a or b]
    far.sort(key=lambda t: -min(t[1], ny - t[1]))
    for a, b in far:
        seg = 1 - sg if a else sg
        at = lax.rem(my + b, ny)
        members.append((seg * ny + at, {"segment": seg, "gy": at}))

    barrier = pltpu.get_barrier_semaphore()
    partners = [peer for _, peer in columns + members]
    partners += [xu, xd, {**xu, "gy": yu}, {**xd, "gy": yd}]
    for peer in partners:
        pl.semaphore_signal(barrier, inc=1, device_id=peer, device_id_type=MESH)

    def deliver(n, ref):
        move = pltpu.make_async_copy(ref, results[n], os.at[n])
        move.start()
        return move

    copies = []

    def send(n, src, dst, peer):
        copy = pltpu.make_async_remote_copy(
            src_ref=src, dst_ref=dst, send_sem=hs.at[n], recv_sem=hr.at[n],
            device_id=peer, device_id_type=MESH,
        )
        copy.start()
        copies.append(copy)
        return copy

    stages = []

    def spread(stage, me, peers, buffer, source):
        for at, peer in peers:
            pltpu.make_async_remote_copy(
                src_ref=source(at), dst_ref=buffer.at[me],
                send_sem=ss.at[stage], recv_sem=rs.at[stage],
                device_id=peer, device_id_type=MESH,
            ).start()
        stages.append((stage, buffer, len(peers) + 1))

    def arrive(stage, buffer, n):
        ref = buffer.at[pl.ds(0, n - 1)]
        pltpu.make_async_copy(ref, ref, rs.at[stage]).wait()

    def add_up(buffer, n):
        part = buffer[0]
        for d in range(1, n):
            part = part + buffer[d]
        return part

    def to_channels(load, xs, yb):
        parts = []
        for h in range(2):
            raw = load(yb * 2 + h).reshape(64, 256)
            d = mm(raw, ta[:, 0:384]).astype(BF)
            parts.append(jnp.concatenate([d[:, 0:128], d[:, 128:256], d[:, 256:384]], axis=0))
        out = mm(ta[:, 384:576], jnp.concatenate(parts, axis=1)).astype(BF)
        for h in range(2):
            start = pl.multiple_of(16 + (yb * 2 + h) * 256, 16)
            a1[xs, pl.ds(start, 256), :] = out[:, h * 128:(h + 1) * 128]

    def own_plane(t, carry):
        x, yb = t // 2, lax.rem(t, 2)

        def load(b):
            return v[:, x, pl.ds(pl.multiple_of(b * 16, 16), 16), :]

        to_channels(load, x + 1, yb)
        return carry

    loads[0].wait()
    loads[1].wait()
    lax.fori_loop(0, 8, own_plane, 0, unroll=UNROLL[0])

    for load in loads[2:]:
        load.wait()

    def eye(n):
        r = lax.broadcasted_iota(jnp.int32, (n, n), 0)
        return r == lax.broadcasted_iota(jnp.int32, (n, n), 1)

    def to_column(row):
        n = row.shape[1]
        return jnp.sum(jnp.where(eye(n), row, 0.0), axis=1, keepdims=True)

    w_tall[...] = jnp.zeros_like(w_tall)
    for t in range(27):
        w_tall[4 * t:4 * t + 4, :] = wh[t].astype(F32)
    w_flat = mm_nt(eye(16).astype(F32).astype(BF), w_tall[...].astype(BF)).astype(BF)
    w1 = jnp.concatenate(
        [mm_nt(w_flat, ta[0:240, 640:768]), mm_nt(w_flat, ta[0:240, 768:896])], axis=0
    ).astype(BF)
    wl[...] = mm_nt(eye(32).astype(F32).astype(BF), wlt[...]).astype(BF)
    b1 = to_column(bh_row[...])
    b1 = jnp.concatenate([b1, b1], axis=0)
    bl = to_column(bl_row[...])

    pl.semaphore_wait(barrier, len(partners))

    c_raw = send(0, v.at[:, 3], halo, xu)
    c_a1y = send(1, a1.at[pl.ds(1, 4), pl.ds(1024, 16)], a1.at[pl.ds(1, 4), pl.ds(0, 16)], {"gy": yu})
    c_a1c = send(2, a1.at[4, pl.ds(1024, 16)], a1.at[0, pl.ds(0, 16)], {**xu, "gy": yu})

    def conv_high(px, t):
        cols = []
        for h in range(2):
            start = pl.multiple_of(t * 128 + h * 64, 16)
            cols.append(jnp.concatenate([a1[2 * px + k, pl.ds(start, 80), :] for k in range(3)], axis=0))
        out = mm(w1, jnp.concatenate(cols, axis=1)) + b1
        acts = (out * sigmoid(out)).astype(BF)
        for h in range(2):
            pre[px, pl.ds(pl.multiple_of(t * 64 + h * 32, 32), 32), :] = out[:, h * 128:(h + 1) * 128]
            start = pl.multiple_of(16 + t * 64 + h * 32, 16)
            act[px + 1, pl.ds(start, 32), :] = acts[:, h * 128:(h + 1) * 128]

    def conv_high_1(t, carry):
        conv_high(1, t)
        return carry

    def conv_high_0(t, carry):
        conv_high(0, t)
        return carry

    lax.fori_loop(1, 8, conv_high_1, 0, unroll=UNROLL[1])
    c_a1y.wait_recv()

    @pl.when(my == 0)
    def _():
        a1[1:5, 0:16, :] = jnp.zeros((4, 16, 128), BF)

    conv_high(1, 0)
    c_ax = send(3, act.at[2, pl.ds(16, 512)], act.at[0, pl.ds(16, 512)], xu)
    c_ac = send(4, act.at[2, pl.ds(512, 16)], act.at[0, pl.ds(0, 16)], {**xu, "gy": yu})
    c_raw.wait_recv()

    @pl.when(first_x)
    def _():
        halo[...] = jnp.zeros_like(halo)

    def halo_plane(yb, carry):
        def load(b):
            return halo[:, pl.ds(pl.multiple_of(b * 16, 16), 16), :]

        to_channels(load, 0, yb)
        return carry

    lax.fori_loop(0, 2, halo_plane, 0, unroll=UNROLL[2])
    c_a1c.wait_recv()

    @pl.when(jnp.logical_or(first_x, my == 0))
    def _():
        a1[0, 0:16, :] = jnp.zeros((16, 128), BF)

    conv_high(0, 7)
    c_ay = send(5, act.at[pl.ds(1, 2), pl.ds(512, 16)], act.at[pl.ds(1, 2), pl.ds(0, 16)], {"gy": yu})
    lax.fori_loop(0, 7, conv_high_0, 0, unroll=UNROLL[1])

    def to_taps(xs, first, count):
        low = act[xs, pl.ds(pl.multiple_of(16 * first, 16), 16 * count), :]
        high = act[xs, pl.ds(pl.multiple_of(256 + 16 * first, 16), 16 * count), :]
        d = mm(jnp.concatenate([low, high], axis=1), tb[:, 0:384]).astype(BF)
        for t in range(count):
            for k in range(3):
                row = pl.multiple_of(((first + t) * 3 + k) * 16, 16)
                taps[xs, pl.ds(row, 16), :] = d[16 * t:16 * (t + 1), 128 * k:128 * (k + 1)]

    def taps_own(t, carry):
        to_taps(1 + t // 4, 1 + 4 * lax.rem(t, 4), 4)
        return carry

    def taps_halo(t, carry):
        to_taps(0, 1 + 4 * t, 4)
        return carry

    lax.fori_loop(0, 8, taps_own, 0, unroll=UNROLL[3])
    c_ay.wait_recv()
    c_ac.wait_recv()

    @pl.when(my == 0)
    def _():
        act[:, 0:16, :] = jnp.zeros((3, 16, 128), BF)

    to_taps(1, 0, 1)
    to_taps(2, 0, 1)
    c_ax.wait_recv()

    @pl.when(first_x)
    def _():
        act[0] = jnp.zeros((528, 128), BF)

    to_taps(0, 0, 1)
    lax.fori_loop(0, 4, taps_halo, 0, unroll=UNROLL[3])

    def window(j):
        start = pl.multiple_of(j * 96, 16)
        return jnp.concatenate([taps[k, pl.ds(start, 144), :] for k in range(3)], axis=0)

    def conv_low(t, total):
        out = mm(wl[...], jnp.concatenate([window(2 * t), window(2 * t + 1)], axis=1)) + bl
        sig = sigmoid(out)
        slopes = (sig * (1.0 + out * (1.0 - sig))).astype(BF)
        values = out * sig
        for h in range(2):
            slope[0, pl.ds(pl.multiple_of(t * 64 + h * 32, 32), 32), :] = slopes[:, h * 128:(h + 1) * 128]
        return total + values[:, :128] + values[:, 128:]

    total = lax.fori_loop(0, 4, conv_low, jnp.zeros((32, 128), F32), unroll=UNROLL[4])

    lane = lax.broadcasted_iota(jnp.int32, (32, 128), 1)
    row = lax.broadcasted_iota(jnp.int32, (32, 128), 0)
    sums = jnp.sum(total, axis=1, keepdims=True)
    mine = jnp.broadcast_to(jnp.sum(jnp.where(lane == row, sums, 0.0), axis=0, keepdims=True), (8, 128))
    pool_s[0] = mine
    pool_1[mx] = mine
    spread(0, mx, columns, pool_1, lambda peer: pool_s.at[0])

    c_sx = send(6, slope.at[0], slope.at[1], xd)
    c_sy = send(7, slope.at[0, pl.ds(0, 32)], slope_y.at[0], {"gy": yd})
    c_sc = send(8, slope.at[0, pl.ds(0, 32)], slope_y.at[1], {**xd, "gy": yd})

    def low_back(t, carry):
        g, gb = carry
        us, ws = [], []
        for h in range(2):
            u = slope[0, pl.ds(pl.multiple_of(t * 64 + h * 32, 32), 32), :]
            us.append(u)
            ws.append(window(2 * t + h))
            gb = gb + u.astype(F32)
        g = g + mm_nt(jnp.concatenate(us, axis=1), jnp.concatenate(ws, axis=1))
        return g, gb

    g_low, gb_low = lax.fori_loop(
        0, 4, low_back, (jnp.zeros((32, 432), F32), jnp.zeros((32, 128), F32)), unroll=UNROLL[5]
    )
    last = jnp.concatenate(
        [g_low[:, 384:432], jnp.sum(gb_low, axis=1, keepdims=True), jnp.zeros((32, 79), F32)], axis=1
    )
    blocks = [g_low[:, 0:128], g_low[:, 128:256], g_low[:, 256:384], last]
    for b in range(4):
        for c in range(4):
            gsend[b * 4 + c] = blocks[c][8 * b:8 * (b + 1), :]
    per = 16 // nx
    g_1[mx] = gsend[pl.ds(mx * per, per)]
    spread(1, mx, columns, g_1, lambda peer: gsend.at[pl.ds(peer * per, per)])

    def spread_rows(px, t):
        u = slope[px, pl.ds(pl.multiple_of(t * 32, 32), 32), :]
        for h in range(2):
            d = mm(u, tb[128 * h:128 * (h + 1), 640:1024]).astype(BF)
            for k in range(3):
                start = pl.multiple_of(((8 * h + t) * 3 + k) * 32, 32)
                up[px, pl.ds(start, 32), :] = d[:, k * 128:(k + 1) * 128]

    def spread_own(t, carry):
        spread_rows(0, t)
        return carry

    def spread_halo(t, carry):
        spread_rows(1, t)
        return carry

    lax.fori_loop(0, 8, spread_own, 0, unroll=UNROLL[6])

    arrive(0, pool_1, nx)
    part = add_up(pool_1, nx)
    pool_s[1] = part
    pool_2[mg] = part
    spread(2, mg, members, pool_2, lambda peer: pool_s.at[1])

    c_sx.wait_recv()
    c_sy.wait_recv()
    c_sc.wait_recv()

    @pl.when(last_x)
    def _():
        slope[1] = jnp.zeros((256, 128), BF)
        slope_y[1] = jnp.zeros((32, 128), BF)

    @pl.when(my == ny - 1)
    def _():
        slope_y[...] = jnp.zeros((2, 32, 128), BF)

    lax.fori_loop(0, 8, spread_halo, 0, unroll=UNROLL[6])
    for px in range(2):
        d = mm(slope_y[px], tb[0:128, 640:1024]).astype(BF)
        for k in range(3):
            up[px, (48 + k) * 32:(49 + k) * 32, :] = d[:, k * 128:(k + 1) * 128]

    def slope_high(t, carry):
        px, yp = t // 8, lax.rem(t, 8)
        at = pl.ds(pl.multiple_of(yp * 64, 64), 64)
        val = pre[px, at, :]
        sig = sigmoid(val)
        pre[px, at, :] = sig * (1.0 + val * (1.0 - sig))
        return carry

    lax.fori_loop(0, 16, slope_high, 0, unroll=UNROLL[7])

    wb[...] = jnp.zeros_like(wb)
    for kx in range(3):
        for ky in range(3):
            for kz in range(3):
                r = (2 * (kx != 1) + (ky != 1)) * 16
                c = (2 * (kx == 0) + (ky == 0)) * 96 + kz * 32
                t = ((kx * 3 + ky) * 3 + kz) * 16
                wb[r:r + 16, c:c + 32] = wlt[t:t + 16, :]

    arrive(1, g_1, nx)
    part = add_up(g_1, nx)
    g_2s[...] = part
    g_2[mg] = part
    spread(3, mg, members, g_2, lambda peer: g_2s)

    arrive(2, pool_2, group)
    part = add_up(pool_2, group)
    scale = 1.0 / cells
    pooled = part[0:1, 0:32] * scale
    weight = hw[...]
    predicted = jnp.sum(weight * pooled, axis=1, keepdims=True) + to_column(hb_row[...])
    error = predicted - to_column(tg_row[...])
    signal = jnp.sum(weight * error, axis=0, keepdims=True)
    head_out[...] = error * pooled
    pred_out[...] = jnp.sum(jnp.where(eye(4), predicted, 0.0), axis=0, keepdims=True)
    weights = (wb[...].astype(F32) * jnp.concatenate([signal] * 12, axis=1)).astype(BF)

    def high_back(t, carry):
        g, gb = carry
        cols = []
        for h in range(2):
            start = pl.multiple_of(t * 192 + h * 96, 32)
            cols.append(jnp.concatenate([up[0, pl.ds(start, 192), :], up[1, pl.ds(start, 192), :]], axis=0))
        out = mm(weights, jnp.concatenate(cols, axis=1)).astype(BF)
        ws, ups = [], []
        for h in range(2):
            at = pl.ds(pl.multiple_of(t * 64 + h * 32, 32), 32)
            begin = pl.multiple_of(t * 128 + h * 64, 16)
            for qx in range(2):
                tile = out[32 * qx:32 * (qx + 1), h * 128:(h + 1) * 128]
                grad_b[qx, at, :] = tile
                u = (tile.astype(F32) * pre[qx, at, :]).astype(BF)
                gb = gb + u.astype(F32)
                ups.append(u)
                ws.append(jnp.concatenate([a1[2 * qx + k, pl.ds(begin, 80), :] for k in range(3)], axis=0))
        g = g + mm_nt(jnp.concatenate(ups, axis=1), jnp.concatenate(ws, axis=1))
        return g, gb

    g_high, gb_high = lax.fori_loop(
        0, 8, high_back, (jnp.zeros((32, 240), F32), jnp.zeros((32, 128), F32)), unroll=UNROLL[8]
    )
    g_w = select(g_high[0:16], ta[0:240, 640:768]) + select(g_high[16:32], ta[0:240, 768:896])
    bias = jnp.sum(gb_high, axis=1, keepdims=True)
    lane16 = lax.broadcasted_iota(jnp.int32, (16, 128), 1)
    h_mine = jnp.where(lane16 == 108, bias[0:16] + bias[16:32], g_w) * scale
    h_s[0] = h_mine
    h_1[mx] = h_mine
    spread(4, mx, columns, h_1, lambda peer: h_s.at[0])

    arrive(3, g_2, group)
    part = add_up(g_2, group)
    g_3[mx] = part
    spread(5, mx, columns, g_3, lambda peer: g_3.at[mx])

    def place(t, carry):
        qx = t // 2
        h = lax.rem(t, 2)
        block = grad_b[qx, pl.ds(pl.multiple_of(h * 256, 256), 256), :]
        out = mm(tb[:, 384:640], block).astype(BF).reshape(16, 16, 128)
        bg_out[:, 2 * sg + qx, pl.ds(pl.multiple_of(h * 16, 16), 16), :] = out
        return carry

    lax.fori_loop(0, 4, place, 0, unroll=UNROLL[9])
    half = bg_out.at[:, pl.ds(2 * sg, 2)]
    c_bg = send(9, half, half, {"segment": 1 - sg})

    arrive(4, h_1, nx)
    part = add_up(h_1, nx)
    h_s[1] = part
    h_2[mg] = part
    spread(6, mg, members, h_2, lambda peer: h_s.at[1])

    arrive(5, g_3, nx)
    bands = []
    for b in range(4):
        bands.append(jnp.concatenate([g_3[(b * 4 + c) // per, (b * 4 + c) % per] for c in range(4)], axis=1))
    g_all = jnp.transpose(jnp.concatenate(bands, axis=0)) * (signal * scale)
    low_out[...] = g_all[0:432, :]
    low_bias[...] = g_all[432:433, :]
    moves = [deliver(n, ref) for n, ref in ((3, low_out), (4, low_bias), (2, head_out), (1, pred_out))]
    c_bg.wait_recv()
    moves.append(deliver(0, bg_out))

    arrive(6, h_2, group)
    h_tall[...] = jnp.transpose(add_up(h_2, group))
    for t in range(27):
        high_out[t] = h_tall[4 * t:4 * t + 4, :]
    high_bias[...] = h_tall[108:109, :]
    moves += [deliver(5, high_out), deliver(6, high_bias)]
    for copy in copies:
        copy.wait_send()
    for stage, buffer, n in stages:
        ref = buffer.at[pl.ds(0, n - 1)]
        pltpu.make_async_copy(ref, ref, ss.at[stage]).wait()
    for move in moves:
        move.wait()


def finish(*refs):
    sources, results, sem = refs[:7], refs[7:14], refs[14]
    pairs = [(sources[0].at[pl.ds(4 * n, 4)], results[0].at[pl.ds(4 * n, 4)]) for n in range(4)]
    pairs += list(zip(sources[1:], results[1:]))
    moves = [pltpu.make_async_copy(a, b, sem.at[n]) for n, (a, b) in enumerate(pairs)]
    for move in moves:
        move.start()
    for move in moves:
        move.wait()


def shards(nx, ny, volume, weight_high, bias_high, weight_low, bias_low, head_weight, head_bias, targets):
    cells = 2 * nx * 16 * ny * 64
    small = (
        jnp.transpose(weight_high, (2, 3, 4, 1, 0)).reshape(27, 4, 16),
        jnp.transpose(weight_low, (2, 3, 4, 1, 0)).reshape(432, 32),
        bias_high[None],
        bias_low[None],
        head_weight.T,
        head_bias[None],
        targets[None],
    )
    tables = [jnp.asarray(t(), BF) for t in (early_tables, late_tables)]
    vm = pl.BlockSpec(memory_space=pltpu.VMEM)
    hbm = pl.BlockSpec(memory_space=pltpu.HBM)
    dma = pltpu.SemaphoreType.DMA
    per = 16 // nx
    group = 2 * ny
    results = (
        jax.ShapeDtypeStruct((16, 4, 32, 128), BF),
        jax.ShapeDtypeStruct((1, 4), F32),
        jax.ShapeDtypeStruct((4, 32), F32),
        jax.ShapeDtypeStruct((432, 32), F32),
        jax.ShapeDtypeStruct((1, 32), F32),
        jax.ShapeDtypeStruct((27, 4, 16), F32),
        jax.ShapeDtypeStruct((1, 16), F32),
    )
    outs = pl.pallas_call(
        functools.partial(kernel, nx, ny, cells),
        out_shape=results,
        in_specs=[hbm] * 10,
        out_specs=(hbm,) * 7,
        scratch_shapes=[
            *(pltpu.VMEM(a.shape, a.dtype) for a in results),
            pltpu.VMEM((4, 4, 64, 256), BF),
            pltpu.VMEM((256, 896), BF),
            pltpu.VMEM((256, 1024), BF),
            *(pltpu.VMEM(a.shape, a.dtype) for a in small),
            pltpu.VMEM((128, 16), F32),
            pltpu.VMEM((32, 432), BF),
            pltpu.VMEM((64, 384), BF),
            pltpu.VMEM((128, 16), F32),
            dma((10,)),
            dma((7,)),
            pltpu.VMEM((4, 64, 256), BF),
            pltpu.VMEM((5, 1040, 128), BF),
            pltpu.VMEM((2, 512, 128), F32),
            pltpu.VMEM((3, 528, 128), BF),
            pltpu.VMEM((3, 816, 128), BF),
            pltpu.VMEM((2, 256, 128), BF),
            pltpu.VMEM((2, 32, 128), BF),
            pltpu.VMEM((2, 1632, 128), BF),
            pltpu.VMEM((2, 512, 128), BF),
            pltpu.VMEM((2, 8, 128), F32),
            pltpu.VMEM((nx, 8, 128), F32),
            pltpu.VMEM((group, 8, 128), F32),
            pltpu.VMEM((16, 8, 128), F32),
            pltpu.VMEM((nx, per, 8, 128), F32),
            pltpu.VMEM((per, 8, 128), F32),
            pltpu.VMEM((group, per, 8, 128), F32),
            pltpu.VMEM((nx, per, 8, 128), F32),
            pltpu.VMEM((2, 16, 128), F32),
            pltpu.VMEM((nx, 16, 128), F32),
            pltpu.VMEM((group, 16, 128), F32),
            dma((10,)), dma((10,)), dma((7,)), dma((7,)),
        ],
        compiler_params=pltpu.CompilerParams(
            collective_id=0, has_side_effects=True, vmem_limit_bytes=64 << 20
        ),
        name="fused",
    )(volume, *tables, *small)
    bg, pred, head, low, low_bias, high, high_bias = pl.pallas_call(
        finish,
        out_shape=results,
        in_specs=[vm] * 7,
        out_specs=(hbm,) * 7,
        scratch_shapes=[dma((10,))],
        compiler_params=pltpu.CompilerParams(vmem_limit_bytes=64 << 20),
        name="finish",
    )(*outs)
    return (
        pred[0],
        bg,
        jnp.transpose(high.reshape(3, 3, 3, 4, 16), (4, 3, 0, 1, 2)),
        high_bias[0],
        jnp.transpose(low.reshape(3, 3, 3, 16, 32), (4, 3, 0, 1, 2)),
        low_bias[0],
        head.T,
    )


def solution(mesh):
    nx, ny = mesh.shape["gx"], mesh.shape["gy"]
    placed = (P(None, "gx", "gy", None), P(), P(), P(), P(), P(), P(), P())
    return jax.shard_map(
        functools.partial(shards, nx, ny),
        mesh=mesh,
        in_specs=placed,
        out_specs=(P(), P(None, "gx", "gy", None), P(), P(), P(), P(), P()),
        check_vma=False,
    )
```

```python
import functools

import jax
import jax.numpy as jnp
import numpy as np
from jax import lax
from jax.experimental import pallas as pl
from jax.experimental.pallas import tpu as pltpu
from jax.sharding import PartitionSpec as P

MESH = pl.DeviceIdType.MESH
BF = jnp.bfloat16
F32 = jnp.float32
UNROLL = (8, 4, 1, 4, 4, 4, 4, 4, 8, 4)


def depth_taps():
    z = np.arange(256)[:, None, None]
    k = np.arange(3)[None, :, None]
    p = np.arange(128)[None, None, :]
    return (z == 2 * p + k - 1).reshape(256, 384)


def rows_to_channels():
    out = np.zeros((16, 16, 12, 16), bool)
    for r in range(12):
        for y in range(16):
            out[y, r, r, y] = True
    return out.reshape(256, 192)


def depth_taps_low():
    out = np.zeros((2, 128, 3, 2, 64), bool)
    for h in range(2):
        for k in range(3):
            for p in range(64):
                if 2 * p + k - 1 >= 0:
                    out[h, 2 * p + k - 1, k, h, p] = True
    return out.reshape(256, 384)


def depth_spread():
    out = np.zeros((2, 64, 2, 3, 128), bool)
    for h in range(2):
        for k in range(3):
            for p in range(64):
                if 2 * p + k - 1 >= 0:
                    out[h, p, h, k, 2 * p + k - 1] = True
    return out.reshape(128, 768)


def channels_to_rows():
    out = np.zeros((16, 16, 16, 16), bool)
    for i in range(16):
        for y in range(16):
            out[i, y, y, i] = True
    return out.reshape(256, 256)


def high_order():
    out = np.zeros((2, 3, 5, 16, 128), bool)
    for s in range(2):
        for kx in range(3):
            for ky in range(3):
                for kz in range(3):
                    for c in range(4):
                        out[s, kx, ky + 2 * s, kz * 4 + c, ((kx * 3 + ky) * 3 + kz) * 4 + c] = True
    return out.reshape(2, 240, 128)


def early_tables():
    out = np.zeros((256, 896), np.float32)
    out[:, 0:384] = depth_taps()
    out[:, 384:576] = rows_to_channels()
    out[0:240, 640:768], out[0:240, 768:896] = high_order()
    return out


def late_tables():
    out = np.zeros((256, 1024), np.float32)
    out[:, 0:384] = depth_taps_low()
    out[:, 384:640] = channels_to_rows()
    spread = depth_spread()
    out[0:128, 640:1024] = spread[:, 0:384]
    out[128:256, 640:1024] = spread[:, 384:768]
    return out


def mm(a, b):
    return lax.dot_general(a, b, (((1,), (0,)), ((), ())), preferred_element_type=F32)


def mm_nt(a, b):
    return lax.dot_general(a, b, (((1,), (1,)), ((), ())), preferred_element_type=F32)


def thirds(x):
    a = x.astype(BF)
    rest = x - a.astype(F32)
    b = rest.astype(BF)
    c = (rest - b.astype(F32)).astype(BF)
    return jnp.concatenate([a, b, c], axis=0)


def select(x, table):
    n = x.shape[0]
    out = mm(thirds(x), table)
    return out[0:n] + out[n:2 * n] + out[2 * n:3 * n]


def sigmoid(x):
    return jax.nn.sigmoid(x)


def kernel(
    nx, ny, cells,
    v_hbm, ta_hbm, tb_hbm, *rest,
):
    small_hbm, results, rest = rest[:7], rest[7:14], rest[14:]
    (
        bg_out, pred_out, head_out, low_out, low_bias, high_out, high_bias,
        v, ta, tb, wh, wlt, bh_row, bl_row, hw, hb_row, tg_row,
        w_tall, wl, wb, h_tall, ls, os,
        halo, a1, pre, act, taps, slope, slope_y, up, grad_b,
        pool_s, pool_1, pool_2, gsend, g_1, g_2s, g_2, g_3, h_s, h_1, h_2,
        hs, hr, ss, rs,
    ) = rest
    sg = lax.axis_index("segment")
    mx = lax.axis_index("gx")
    my = lax.axis_index("gy")
    group = 2 * ny
    mg = sg * ny + my
    yu, yd = lax.rem(my + 1, ny), lax.rem(my + ny - 1, ny)
    xu = {"segment": 1 - sg, "gx": lax.rem(mx + sg, nx)}
    xd = {"segment": 1 - sg, "gx": lax.rem(mx + nx - 1 + sg, nx)}
    first_x = jnp.logical_and(mx == 0, sg == 0)
    last_x = jnp.logical_and(mx == nx - 1, sg == 1)

    loads = [
        pltpu.make_async_copy(v_hbm.at[:, pl.ds(4 * sg, 4)], v, ls.at[0]),
        pltpu.make_async_copy(ta_hbm, ta, ls.at[1]),
    ]
    for n, (src, dst) in enumerate(zip(small_hbm, (wh, wlt, bh_row, bl_row, hw, hb_row, tg_row))):
        loads.append(pltpu.make_async_copy(src, dst, ls.at[2 + n]))
    loads.append(pltpu.make_async_copy(tb_hbm, tb, ls.at[9]))
    for load in loads:
        load.start()

    columns, members = [], []
    if nx == 16:
        far = [(a, b) for a in range(4) for b in range(4) if a or b]
        far.sort(key=lambda t: -min(t[0], 4 - t[0]) - min(t[1], 4 - t[1]))
        for a, b in far:
            at = lax.rem(mx // 4 + a, 4) * 4 + lax.rem(lax.rem(mx, 4) + b, 4)
            columns.append((at, {"gx": at}))
    else:
        for d in range(1, nx):
            at = lax.rem(mx + d, nx)
            columns.append((at, {"gx": at}))
    far = [(a, b) for a in range(2) for b in range(ny) if a or b]
    far.sort(key=lambda t: -min(t[1], ny - t[1]))
    for a, b in far:
        seg = 1 - sg if a else sg
        at = lax.rem(my + b, ny)
        members.append((seg * ny + at, {"segment": seg, "gy": at}))

    barrier = pltpu.get_barrier_semaphore()
    partners = [peer for _, peer in columns + members]
    partners += [xu, xd, {**xu, "gy": yu}, {**xd, "gy": yd}]
    for peer in partners:
        pl.semaphore_signal(barrier, inc=1, device_id=peer, device_id_type=MESH)

    def deliver(n, ref):
        move = pltpu.make_async_copy(ref, results[n], os.at[n])
        move.start()
        return move

    copies = []

    def send(n, src, dst, peer):
        copy = pltpu.make_async_remote_copy(
            src_ref=src, dst_ref=dst, send_sem=hs.at[n], recv_sem=hr.at[n],
            device_id=peer, device_id_type=MESH,
        )
        copy.start()
        copies.append(copy)
        return copy

    stages = []

    def spread(stage, me, peers, buffer, source):
        for at, peer in peers:
            pltpu.make_async_remote_copy(
                src_ref=source(at), dst_ref=buffer.at[me],
                send_sem=ss.at[stage], recv_sem=rs.at[stage],
                device_id=peer, device_id_type=MESH,
            ).start()
        stages.append((stage, buffer, len(peers) + 1))

    def arrive(stage, buffer, n):
        ref = buffer.at[pl.ds(0, n - 1)]
        pltpu.make_async_copy(ref, ref, rs.at[stage]).wait()

    def add_up(buffer, n):
        part = buffer[0]
        for d in range(1, n):
            part = part + buffer[d]
        return part

    def to_channels(load, xs, yb):
        parts = []
        for h in range(2):
            raw = load(yb * 2 + h).reshape(64, 256)
            d = mm(raw, ta[:, 0:384]).astype(BF)
            parts.append(jnp.concatenate([d[:, 0:128], d[:, 128:256], d[:, 256:384]], axis=0))
        out = mm(ta[:, 384:576], jnp.concatenate(parts, axis=1)).astype(BF)
        for h in range(2):
            start = pl.multiple_of(48 + (yb * 2 + h) * 256, 16)
            a1[xs, pl.ds(start, 256), :] = out[:, h * 128:(h + 1) * 128]

    def own_plane(t, carry):
        x, yb = t // 2, lax.rem(t, 2)

        def load(b):
            return v[:, x, pl.ds(pl.multiple_of(b * 16, 16), 16), :]

        to_channels(load, x + 1, yb)
        return carry

    loads[0].wait()
    loads[1].wait()
    lax.fori_loop(0, 8, own_plane, 0, unroll=UNROLL[0])

    for load in loads[2:]:
        load.wait()

    def eye(n):
        r = lax.broadcasted_iota(jnp.int32, (n, n), 0)
        return r == lax.broadcasted_iota(jnp.int32, (n, n), 1)

    def to_column(row):
        n = row.shape[1]
        return jnp.sum(jnp.where(eye(n), row, 0.0), axis=1, keepdims=True)

    w_tall[...] = jnp.zeros_like(w_tall)
    for t in range(27):
        w_tall[4 * t:4 * t + 4, :] = wh[t].astype(F32)
    w_flat = mm_nt(eye(16).astype(F32).astype(BF), w_tall[...].astype(BF)).astype(BF)
    w1 = jnp.concatenate(
        [mm_nt(w_flat, ta[0:240, 640:768]), mm_nt(w_flat, ta[0:240, 768:896])], axis=0
    ).astype(BF)
    wl[...] = mm_nt(eye(32).astype(F32).astype(BF), wlt[...]).astype(BF)
    b1 = to_column(bh_row[...])
    b1 = jnp.concatenate([b1, b1], axis=0)
    bl = to_column(bl_row[...])

    pl.semaphore_wait(barrier, len(partners))

    c_raw = [
        send(5 * n, v.at[:, 3, pl.ds(32 * n, 32)], halo.at[:, pl.ds(32 * n, 32)], xu) for n in range(2)
    ]
    c_a1y = send(1, a1.at[pl.ds(1, 4), pl.ds(1024, 48)], a1.at[pl.ds(1, 4), pl.ds(0, 48)], {"gy": yu})
    c_a1c = send(2, a1.at[4, pl.ds(1024, 48)], a1.at[0, pl.ds(0, 48)], {**xu, "gy": yu})

    def conv_high(px, t):
        cols = []
        for h in range(2):
            start = pl.multiple_of(32 + t * 128 + h * 64, 16)
            cols.append(jnp.concatenate([a1[2 * px + k, pl.ds(start, 80), :] for k in range(3)], axis=0))
        out = mm(w1, jnp.concatenate(cols, axis=1)) + b1
        acts = (out * sigmoid(out)).astype(BF)
        for h in range(2):
            pre[px, pl.ds(pl.multiple_of(t * 64 + h * 32, 32), 32), :] = out[:, h * 128:(h + 1) * 128]
            start = pl.multiple_of(16 + t * 64 + h * 32, 16)
            act[px + 1, pl.ds(start, 32), :] = acts[:, h * 128:(h + 1) * 128]

    def conv_edge(px):
        cols = jnp.concatenate([a1[2 * px + k, 0:80, :] for k in range(3)], axis=0)
        out = (mm(w1, cols) + b1)[0:16]
        acts = (out * sigmoid(out)).astype(BF)
        act[px + 1, 0:16, :] = jnp.where(my == 0, jnp.zeros_like(acts), acts)

    def conv_high_1(t, carry):
        conv_high(1, t)
        return carry

    def conv_high_0(t, carry):
        conv_high(0, t)
        return carry

    def to_taps(xs, first, count):
        low = act[xs, pl.ds(pl.multiple_of(16 * first, 16), 16 * count), :]
        high = act[xs, pl.ds(pl.multiple_of(256 + 16 * first, 16), 16 * count), :]
        d = mm(jnp.concatenate([low, high], axis=1), tb[:, 0:384]).astype(BF)
        for t in range(count):
            for k in range(3):
                row = pl.multiple_of(((first + t) * 3 + k) * 16, 16)
                taps[xs, pl.ds(row, 16), :] = d[16 * t:16 * (t + 1), 128 * k:128 * (k + 1)]

    def all_taps(xs):
        def body(t, carry):
            to_taps(xs, 1 + 4 * t, 4)
            return carry

        lax.fori_loop(0, 4, body, 0, unroll=UNROLL[3])
        to_taps(xs, 0, 1)

    lax.fori_loop(1, 8, conv_high_1, 0, unroll=UNROLL[1])
    c_ax = [send(3, act.at[2, pl.ds(80, 448)], act.at[0, pl.ds(80, 448)], xu)]
    c_a1y.wait_recv()

    @pl.when(my == 0)
    def _():
        a1[1:5, 0:48, :] = jnp.zeros((4, 48, 128), BF)

    conv_high(1, 0)
    conv_edge(1)
    c_ax.append(send(4, act.at[2, pl.ds(0, 80)], act.at[0, pl.ds(0, 80)], xu))
    all_taps(2)
    c_a1c.wait_recv()

    @pl.when(jnp.logical_or(first_x, my == 0))
    def _():
        a1[0, 0:48, :] = jnp.zeros((48, 128), BF)

    for n in range(2):
        c_raw[n].wait_recv()

        @pl.when(first_x)
        def _():
            halo[:, 32 * n:32 * n + 32, :] = jnp.zeros((4, 32, 256), BF)

        def load(b):
            return halo[:, 16 * b:16 * b + 16, :]

        to_channels(load, 0, n)
        lax.fori_loop(4 * n, 4 * n + 4, conv_high_0, 0, unroll=UNROLL[1])
    conv_edge(0)
    all_taps(1)
    for copy in c_ax:
        copy.wait_recv()

    @pl.when(first_x)
    def _():
        act[0] = jnp.zeros((528, 128), BF)

    all_taps(0)

    def window(j):
        start = pl.multiple_of(j * 96, 16)
        return jnp.concatenate([taps[k, pl.ds(start, 144), :] for k in range(3)], axis=0)

    def conv_low(t, total):
        out = mm(wl[...], jnp.concatenate([window(2 * t), window(2 * t + 1)], axis=1)) + bl
        sig = sigmoid(out)
        slopes = (sig * (1.0 + out * (1.0 - sig))).astype(BF)
        values = out * sig
        for h in range(2):
            slope[0, pl.ds(pl.multiple_of(t * 64 + h * 32, 32), 32), :] = slopes[:, h * 128:(h + 1) * 128]
        return total + values[:, :128] + values[:, 128:]

    total = lax.fori_loop(0, 4, conv_low, jnp.zeros((32, 128), F32), unroll=UNROLL[4])

    lane = lax.broadcasted_iota(jnp.int32, (32, 128), 1)
    row = lax.broadcasted_iota(jnp.int32, (32, 128), 0)
    sums = jnp.sum(total, axis=1, keepdims=True)
    mine = jnp.broadcast_to(jnp.sum(jnp.where(lane == row, sums, 0.0), axis=0, keepdims=True), (8, 128))
    pool_s[0] = mine
    pool_1[mx] = mine
    spread(0, mx, columns, pool_1, lambda peer: pool_s.at[0])

    c_sx = send(6, slope.at[0], slope.at[1], xd)
    c_sy = send(7, slope.at[0, pl.ds(0, 32)], slope_y.at[0], {"gy": yd})
    c_sc = send(8, slope.at[0, pl.ds(0, 32)], slope_y.at[1], {**xd, "gy": yd})

    def low_back(t, carry):
        g, gb = carry
        us, ws = [], []
        for h in range(2):
            u = slope[0, pl.ds(pl.multiple_of(t * 64 + h * 32, 32), 32), :]
            us.append(u)
            ws.append(window(2 * t + h))
            gb = gb + u.astype(F32)
        g = g + mm_nt(jnp.concatenate(us, axis=1), jnp.concatenate(ws, axis=1))
        return g, gb

    g_low, gb_low = lax.fori_loop(
        0, 4, low_back, (jnp.zeros((32, 432), F32), jnp.zeros((32, 128), F32)), unroll=UNROLL[5]
    )
    last = jnp.concatenate(
        [g_low[:, 384:432], jnp.sum(gb_low, axis=1, keepdims=True), jnp.zeros((32, 79), F32)], axis=1
    )
    blocks = [g_low[:, 0:128], g_low[:, 128:256], g_low[:, 256:384], last]
    for b in range(4):
        for c in range(4):
            gsend[b * 4 + c] = blocks[c][8 * b:8 * (b + 1), :]
    per = 16 // nx
    g_1[mx] = gsend[pl.ds(mx * per, per)]
    spread(1, mx, columns, g_1, lambda peer: gsend.at[pl.ds(peer * per, per)])

    def spread_rows(px, t):
        u = slope[px, pl.ds(pl.multiple_of(t * 32, 32), 32), :]
        for h in range(2):
            d = mm(u, tb[128 * h:128 * (h + 1), 640:1024]).astype(BF)
            for k in range(3):
                start = pl.multiple_of(((8 * h + t) * 3 + k) * 32, 32)
                up[px, pl.ds(start, 32), :] = d[:, k * 128:(k + 1) * 128]

    def spread_own(t, carry):
        spread_rows(0, t)
        return carry

    def spread_halo(t, carry):
        spread_rows(1, t)
        return carry

    lax.fori_loop(0, 8, spread_own, 0, unroll=UNROLL[6])

    arrive(0, pool_1, nx)
    part = add_up(pool_1, nx)
    pool_s[1] = part
    pool_2[mg] = part
    spread(2, mg, members, pool_2, lambda peer: pool_s.at[1])

    c_sx.wait_recv()
    c_sy.wait_recv()
    c_sc.wait_recv()

    @pl.when(last_x)
    def _():
        slope[1] = jnp.zeros((256, 128), BF)
        slope_y[1] = jnp.zeros((32, 128), BF)

    @pl.when(my == ny - 1)
    def _():
        slope_y[...] = jnp.zeros((2, 32, 128), BF)

    lax.fori_loop(0, 8, spread_halo, 0, unroll=UNROLL[6])
    for px in range(2):
        d = mm(slope_y[px], tb[0:128, 640:1024]).astype(BF)
        for k in range(3):
            up[px, (48 + k) * 32:(49 + k) * 32, :] = d[:, k * 128:(k + 1) * 128]

    def slope_high(t, carry):
        px, yp = t // 8, lax.rem(t, 8)
        at = pl.ds(pl.multiple_of(yp * 64, 64), 64)
        val = pre[px, at, :]
        sig = sigmoid(val)
        pre[px, at, :] = sig * (1.0 + val * (1.0 - sig))
        return carry

    lax.fori_loop(0, 16, slope_high, 0, unroll=UNROLL[7])

    wb[...] = jnp.zeros_like(wb)
    for kx in range(3):
        for ky in range(3):
            for kz in range(3):
                r = (2 * (kx != 1) + (ky != 1)) * 16
                c = (2 * (kx == 0) + (ky == 0)) * 96 + kz * 32
                t = ((kx * 3 + ky) * 3 + kz) * 16
                wb[r:r + 16, c:c + 32] = wlt[t:t + 16, :]

    arrive(1, g_1, nx)
    part = add_up(g_1, nx)
    g_2s[...] = part
    g_2[mg] = part
    spread(3, mg, members, g_2, lambda peer: g_2s)

    arrive(2, pool_2, group)
    part = add_up(pool_2, group)
    scale = 1.0 / cells
    pooled = part[0:1, 0:32] * scale
    weight = hw[...]
    predicted = jnp.sum(weight * pooled, axis=1, keepdims=True) + to_column(hb_row[...])
    error = predicted - to_column(tg_row[...])
    signal = jnp.sum(weight * error, axis=0, keepdims=True)
    head_out[...] = error * pooled
    pred_out[...] = jnp.sum(jnp.where(eye(4), predicted, 0.0), axis=0, keepdims=True)
    weights = (wb[...].astype(F32) * jnp.concatenate([signal] * 12, axis=1)).astype(BF)

    def high_back(t, carry):
        g, gb = carry
        cols = []
        for h in range(2):
            start = pl.multiple_of(t * 192 + h * 96, 32)
            cols.append(jnp.concatenate([up[0, pl.ds(start, 192), :], up[1, pl.ds(start, 192), :]], axis=0))
        out = mm(weights, jnp.concatenate(cols, axis=1)).astype(BF)
        ws, ups = [], []
        for h in range(2):
            at = pl.ds(pl.multiple_of(t * 64 + h * 32, 32), 32)
            begin = pl.multiple_of(32 + t * 128 + h * 64, 16)
            for qx in range(2):
                tile = out[32 * qx:32 * (qx + 1), h * 128:(h + 1) * 128]
                grad_b[qx, at, :] = tile
                u = (tile.astype(F32) * pre[qx, at, :]).astype(BF)
                gb = gb + u.astype(F32)
                ups.append(u)
                ws.append(jnp.concatenate([a1[2 * qx + k, pl.ds(begin, 80), :] for k in range(3)], axis=0))
        g = g + mm_nt(jnp.concatenate(ups, axis=1), jnp.concatenate(ws, axis=1))
        return g, gb

    g_high, gb_high = lax.fori_loop(
        0, 8, high_back, (jnp.zeros((32, 240), F32), jnp.zeros((32, 128), F32)), unroll=UNROLL[8]
    )
    g_w = select(g_high[0:16], ta[0:240, 640:768]) + select(g_high[16:32], ta[0:240, 768:896])
    bias = jnp.sum(gb_high, axis=1, keepdims=True)
    lane16 = lax.broadcasted_iota(jnp.int32, (16, 128), 1)
    h_mine = jnp.where(lane16 == 108, bias[0:16] + bias[16:32], g_w) * scale
    h_s[0] = h_mine
    h_1[mx] = h_mine
    spread(4, mx, columns, h_1, lambda peer: h_s.at[0])

    arrive(3, g_2, group)
    part = add_up(g_2, group)
    g_3[mx] = part
    spread(5, mx, columns, g_3, lambda peer: g_3.at[mx])

    def place(t, carry):
        qx = t // 2
        h = lax.rem(t, 2)
        block = grad_b[qx, pl.ds(pl.multiple_of(h * 256, 256), 256), :]
        out = mm(tb[:, 384:640], block).astype(BF).reshape(16, 16, 128)
        bg_out[:, 2 * sg + qx, pl.ds(pl.multiple_of(h * 16, 16), 16), :] = out
        return carry

    lax.fori_loop(0, 4, place, 0, unroll=UNROLL[9])
    half = bg_out.at[:, pl.ds(2 * sg, 2)]
    c_bg = send(9, half, half, {"segment": 1 - sg})

    arrive(4, h_1, nx)
    part = add_up(h_1, nx)
    h_s[1] = part
    h_2[mg] = part
    spread(6, mg, members, h_2, lambda peer: h_s.at[1])

    arrive(5, g_3, nx)
    bands = []
    for b in range(4):
        bands.append(jnp.concatenate([g_3[(b * 4 + c) // per, (b * 4 + c) % per] for c in range(4)], axis=1))
    g_all = jnp.transpose(jnp.concatenate(bands, axis=0)) * (signal * scale)
    low_out[...] = g_all[0:432, :]
    low_bias[...] = g_all[432:433, :]
    moves = [deliver(n, ref) for n, ref in ((3, low_out), (4, low_bias), (2, head_out), (1, pred_out))]
    c_bg.wait_recv()
    moves.append(deliver(0, bg_out))

    arrive(6, h_2, group)
    h_tall[...] = jnp.transpose(add_up(h_2, group))
    for t in range(27):
        high_out[t] = h_tall[4 * t:4 * t + 4, :]
    high_bias[...] = h_tall[108:109, :]
    moves += [deliver(5, high_out), deliver(6, high_bias)]
    for copy in copies:
        copy.wait_send()
    for stage, buffer, n in stages:
        ref = buffer.at[pl.ds(0, n - 1)]
        pltpu.make_async_copy(ref, ref, ss.at[stage]).wait()
    for move in moves:
        move.wait()


def finish(*refs):
    sources, results, sem = refs[:7], refs[7:14], refs[14]
    pairs = [(sources[0].at[pl.ds(4 * n, 4)], results[0].at[pl.ds(4 * n, 4)]) for n in range(4)]
    pairs += list(zip(sources[1:], results[1:]))
    moves = [pltpu.make_async_copy(a, b, sem.at[n]) for n, (a, b) in enumerate(pairs)]
    for move in moves:
        move.start()
    for move in moves:
        move.wait()


def shards(nx, ny, volume, weight_high, bias_high, weight_low, bias_low, head_weight, head_bias, targets):
    cells = 2 * nx * 16 * ny * 64
    small = (
        jnp.transpose(weight_high, (2, 3, 4, 1, 0)).reshape(27, 4, 16),
        jnp.transpose(weight_low, (2, 3, 4, 1, 0)).reshape(432, 32),
        bias_high[None],
        bias_low[None],
        head_weight.T,
        head_bias[None],
        targets[None],
    )
    tables = [jnp.asarray(t(), BF) for t in (early_tables, late_tables)]
    vm = pl.BlockSpec(memory_space=pltpu.VMEM)
    hbm = pl.BlockSpec(memory_space=pltpu.HBM)
    dma = pltpu.SemaphoreType.DMA
    per = 16 // nx
    group = 2 * ny
    results = (
        jax.ShapeDtypeStruct((16, 4, 32, 128), BF),
        jax.ShapeDtypeStruct((1, 4), F32),
        jax.ShapeDtypeStruct((4, 32), F32),
        jax.ShapeDtypeStruct((432, 32), F32),
        jax.ShapeDtypeStruct((1, 32), F32),
        jax.ShapeDtypeStruct((27, 4, 16), F32),
        jax.ShapeDtypeStruct((1, 16), F32),
    )
    outs = pl.pallas_call(
        functools.partial(kernel, nx, ny, cells),
        out_shape=results,
        in_specs=[hbm] * 10,
        out_specs=(hbm,) * 7,
        scratch_shapes=[
            *(pltpu.VMEM(a.shape, a.dtype) for a in results),
            pltpu.VMEM((4, 4, 64, 256), BF),
            pltpu.VMEM((256, 896), BF),
            pltpu.VMEM((256, 1024), BF),
            *(pltpu.VMEM(a.shape, a.dtype) for a in small),
            pltpu.VMEM((128, 16), F32),
            pltpu.VMEM((32, 432), BF),
            pltpu.VMEM((64, 384), BF),
            pltpu.VMEM((128, 16), F32),
            dma((10,)),
            dma((7,)),
            pltpu.VMEM((4, 64, 256), BF),
            pltpu.VMEM((5, 1072, 128), BF),
            pltpu.VMEM((2, 512, 128), F32),
            pltpu.VMEM((3, 528, 128), BF),
            pltpu.VMEM((3, 816, 128), BF),
            pltpu.VMEM((2, 256, 128), BF),
            pltpu.VMEM((2, 32, 128), BF),
            pltpu.VMEM((2, 1632, 128), BF),
            pltpu.VMEM((2, 512, 128), BF),
            pltpu.VMEM((2, 8, 128), F32),
            pltpu.VMEM((nx, 8, 128), F32),
            pltpu.VMEM((group, 8, 128), F32),
            pltpu.VMEM((16, 8, 128), F32),
            pltpu.VMEM((nx, per, 8, 128), F32),
            pltpu.VMEM((per, 8, 128), F32),
            pltpu.VMEM((group, per, 8, 128), F32),
            pltpu.VMEM((nx, per, 8, 128), F32),
            pltpu.VMEM((2, 16, 128), F32),
            pltpu.VMEM((nx, 16, 128), F32),
            pltpu.VMEM((group, 16, 128), F32),
            dma((10,)), dma((10,)), dma((7,)), dma((7,)),
        ],
        compiler_params=pltpu.CompilerParams(
            collective_id=0, has_side_effects=True, vmem_limit_bytes=64 << 20
        ),
        name="fused",
    )(volume, *tables, *small)
    bg, pred, head, low, low_bias, high, high_bias = pl.pallas_call(
        finish,
        out_shape=results,
        in_specs=[vm] * 7,
        out_specs=(hbm,) * 7,
        scratch_shapes=[dma((10,))],
        compiler_params=pltpu.CompilerParams(vmem_limit_bytes=64 << 20),
        name="finish",
    )(*outs)
    return (
        pred[0],
        bg,
        jnp.transpose(high.reshape(3, 3, 3, 4, 16), (4, 3, 0, 1, 2)),
        high_bias[0],
        jnp.transpose(low.reshape(3, 3, 3, 16, 32), (4, 3, 0, 1, 2)),
        low_bias[0],
        head.T,
    )


def solution(mesh):
    nx, ny = mesh.shape["gx"], mesh.shape["gy"]
    placed = (P(None, "gx", "gy", None), P(), P(), P(), P(), P(), P(), P())
    return jax.shard_map(
        functools.partial(shards, nx, ny),
        mesh=mesh,
        in_specs=placed,
        out_specs=(P(), P(None, "gx", "gy", None), P(), P(), P(), P(), P()),
        check_vma=False,
    )
```

```python
import functools

import jax
import jax.numpy as jnp
import numpy as np
from jax import lax
from jax.experimental import pallas as pl
from jax.experimental.pallas import tpu as pltpu
from jax.sharding import PartitionSpec as P

MESH = pl.DeviceIdType.MESH
BF = jnp.bfloat16
F32 = jnp.float32
UNROLL = (8, 4, 1, 4, 4, 4, 4, 4, 8, 4)


def depth_taps():
    z = np.arange(256)[:, None, None]
    k = np.arange(3)[None, :, None]
    p = np.arange(128)[None, None, :]
    return (z == 2 * p + k - 1).reshape(256, 384)


def rows_to_channels():
    out = np.zeros((16, 16, 12, 16), bool)
    for r in range(12):
        for y in range(16):
            out[y, r, r, y] = True
    return out.reshape(256, 192)


def depth_taps_low():
    out = np.zeros((2, 128, 3, 2, 64), bool)
    for h in range(2):
        for k in range(3):
            for p in range(64):
                if 2 * p + k - 1 >= 0:
                    out[h, 2 * p + k - 1, k, h, p] = True
    return out.reshape(256, 384)


def depth_spread():
    out = np.zeros((2, 64, 2, 3, 128), bool)
    for h in range(2):
        for k in range(3):
            for p in range(64):
                if 2 * p + k - 1 >= 0:
                    out[h, p, h, k, 2 * p + k - 1] = True
    return out.reshape(128, 768)


def channels_to_rows():
    out = np.zeros((16, 16, 16, 16), bool)
    for i in range(16):
        for y in range(16):
            out[i, y, y, i] = True
    return out.reshape(256, 256)


def high_order():
    out = np.zeros((2, 3, 5, 16, 128), bool)
    for s in range(2):
        for kx in range(3):
            for ky in range(3):
                for kz in range(3):
                    for c in range(4):
                        out[s, kx, ky + 2 * s, kz * 4 + c, ((kx * 3 + ky) * 3 + kz) * 4 + c] = True
    return out.reshape(2, 240, 128)


def early_tables():
    out = np.zeros((256, 896), np.float32)
    out[:, 0:384] = depth_taps()
    out[:, 384:576] = rows_to_channels()
    out[0:240, 640:768], out[0:240, 768:896] = high_order()
    return out


def late_tables():
    out = np.zeros((256, 1024), np.float32)
    out[:, 0:384] = depth_taps_low()
    out[:, 384:640] = channels_to_rows()
    spread = depth_spread()
    out[0:128, 640:1024] = spread[:, 0:384]
    out[128:256, 640:1024] = spread[:, 384:768]
    return out


def mm(a, b):
    return lax.dot_general(a, b, (((1,), (0,)), ((), ())), preferred_element_type=F32)


def mm_nt(a, b):
    return lax.dot_general(a, b, (((1,), (1,)), ((), ())), preferred_element_type=F32)


def thirds(x):
    a = x.astype(BF)
    rest = x - a.astype(F32)
    b = rest.astype(BF)
    c = (rest - b.astype(F32)).astype(BF)
    return jnp.concatenate([a, b, c], axis=0)


def select(x, table):
    n = x.shape[0]
    out = mm(thirds(x), table)
    return out[0:n] + out[n:2 * n] + out[2 * n:3 * n]


def sigmoid(x):
    return jax.nn.sigmoid(x)


def kernel(
    nx, ny, cells,
    v_hbm, ta_hbm, tb_hbm, *rest,
):
    small_hbm, results, rest = rest[:7], rest[7:14], rest[14:]
    (
        bg_out, pred_out, head_out, low_out, low_bias, high_out, high_bias,
        v, ta, tb, wh, wlt, bh_row, bl_row, hw, hb_row, tg_row,
        w_tall, wl, wb, h_tall, ls, os,
        halo, a1, pre, act, taps, slope, slope_y, up, grad_b,
        pool_s, pool_1, pool_2, gsend, g_1, g_2s, g_2, g_3, h_s, h_1, h_2,
        hs, hr, ss, rs,
    ) = rest
    sg = lax.axis_index("segment")
    mx = lax.axis_index("gx")
    my = lax.axis_index("gy")
    group = 2 * ny
    mg = sg * ny + my
    yu, yd = lax.rem(my + 1, ny), lax.rem(my + ny - 1, ny)
    xu = {"segment": 1 - sg, "gx": lax.rem(mx + sg, nx)}
    xd = {"segment": 1 - sg, "gx": lax.rem(mx + nx - 1 + sg, nx)}
    first_x = jnp.logical_and(mx == 0, sg == 0)
    last_x = jnp.logical_and(mx == nx - 1, sg == 1)

    loads = [
        pltpu.make_async_copy(v_hbm.at[:, pl.ds(4 * sg, 4)], v, ls.at[0]),
        pltpu.make_async_copy(ta_hbm, ta, ls.at[1]),
    ]
    for n, (src, dst) in enumerate(zip(small_hbm, (wh, wlt, bh_row, bl_row, hw, hb_row, tg_row))):
        loads.append(pltpu.make_async_copy(src, dst, ls.at[2 + n]))
    loads.append(pltpu.make_async_copy(tb_hbm, tb, ls.at[9]))
    for load in loads:
        load.start()

    columns, members = [], []
    if nx == 16:
        far = [(a, b) for a in range(4) for b in range(4) if a or b]
        far.sort(key=lambda t: -min(t[0], 4 - t[0]) - min(t[1], 4 - t[1]))
        for a, b in far:
            at = lax.rem(mx // 4 + a, 4) * 4 + lax.rem(lax.rem(mx, 4) + b, 4)
            columns.append((at, {"gx": at}))
    else:
        for d in range(1, nx):
            at = lax.rem(mx + d, nx)
            columns.append((at, {"gx": at}))
    far = [(a, b) for a in range(2) for b in range(ny) if a or b]
    far.sort(key=lambda t: -min(t[1], ny - t[1]))
    for a, b in far:
        seg = 1 - sg if a else sg
        at = lax.rem(my + b, ny)
        members.append((seg * ny + at, {"segment": seg, "gy": at}))

    barrier = pltpu.get_barrier_semaphore()
    partners = [peer for _, peer in members + columns]
    partners += [xu, xd, {**xu, "gy": yu}, {**xd, "gy": yd}]
    for peer in partners:
        pl.semaphore_signal(barrier, inc=1, device_id=peer, device_id_type=MESH)

    def deliver(n, ref):
        move = pltpu.make_async_copy(ref, results[n], os.at[n])
        move.start()
        return move

    copies = []

    def send(n, src, dst, peer):
        copy = pltpu.make_async_remote_copy(
            src_ref=src, dst_ref=dst, send_sem=hs.at[n], recv_sem=hr.at[n],
            device_id=peer, device_id_type=MESH,
        )
        copy.start()
        copies.append(copy)
        return copy

    stages = []

    def spread(stage, me, peers, buffer, source):
        for at, peer in peers:
            pltpu.make_async_remote_copy(
                src_ref=source(at), dst_ref=buffer.at[me],
                send_sem=ss.at[stage], recv_sem=rs.at[stage],
                device_id=peer, device_id_type=MESH,
            ).start()
        stages.append((stage, buffer, len(peers) + 1))

    def arrive(stage, buffer, n):
        ref = buffer.at[pl.ds(0, n - 1)]
        pltpu.make_async_copy(ref, ref, rs.at[stage]).wait()

    def add_up(buffer, n):
        part = buffer[0]
        for d in range(1, n):
            part = part + buffer[d]
        return part

    def to_channels(load, xs, yb):
        parts = []
        for h in range(2):
            raw = load(yb * 2 + h).reshape(64, 256)
            d = mm(raw, ta[:, 0:384]).astype(BF)
            parts.append(jnp.concatenate([d[:, 0:128], d[:, 128:256], d[:, 256:384]], axis=0))
        out = mm(ta[:, 384:576], jnp.concatenate(parts, axis=1)).astype(BF)
        for h in range(2):
            start = pl.multiple_of(48 + (yb * 2 + h) * 256, 16)
            a1[xs, pl.ds(start, 256), :] = out[:, h * 128:(h + 1) * 128]

    def own_plane(t, carry):
        x, yb = t // 2, lax.rem(t, 2)

        def load(b):
            return v[:, x, pl.ds(pl.multiple_of(b * 16, 16), 16), :]

        to_channels(load, x + 1, yb)
        return carry

    loads[0].wait()
    loads[1].wait()
    lax.fori_loop(0, 8, own_plane, 0, unroll=UNROLL[0])

    pl.semaphore_wait(barrier, len(partners))

    c_raw = [
        send(5 * n, v.at[:, 3, pl.ds(32 * n, 32)], halo.at[:, pl.ds(32 * n, 32)], xu) for n in range(2)
    ]
    c_a1y = send(1, a1.at[pl.ds(1, 4), pl.ds(1024, 48)], a1.at[pl.ds(1, 4), pl.ds(0, 48)], {"gy": yu})
    c_a1c = send(2, a1.at[4, pl.ds(1024, 48)], a1.at[0, pl.ds(0, 48)], {**xu, "gy": yu})

    for load in loads[2:]:
        load.wait()

    def eye(n):
        r = lax.broadcasted_iota(jnp.int32, (n, n), 0)
        return r == lax.broadcasted_iota(jnp.int32, (n, n), 1)

    def to_column(row):
        n = row.shape[1]
        return jnp.sum(jnp.where(eye(n), row, 0.0), axis=1, keepdims=True)

    w_tall[...] = jnp.zeros_like(w_tall)
    for t in range(27):
        w_tall[4 * t:4 * t + 4, :] = wh[t].astype(F32)
    w_flat = mm_nt(eye(16).astype(F32).astype(BF), w_tall[...].astype(BF)).astype(BF)
    w1 = jnp.concatenate(
        [mm_nt(w_flat, ta[0:240, 640:768]), mm_nt(w_flat, ta[0:240, 768:896])], axis=0
    ).astype(BF)
    wl[...] = mm_nt(eye(32).astype(F32).astype(BF), wlt[...]).astype(BF)
    b1 = to_column(bh_row[...])
    b1 = jnp.concatenate([b1, b1], axis=0)
    bl = to_column(bl_row[...])

    def conv_high(px, t):
        cols = []
        for h in range(2):
            start = pl.multiple_of(32 + t * 128 + h * 64, 16)
            cols.append(jnp.concatenate([a1[2 * px + k, pl.ds(start, 80), :] for k in range(3)], axis=0))
        out = mm(w1, jnp.concatenate(cols, axis=1)) + b1
        acts = (out * sigmoid(out)).astype(BF)
        for h in range(2):
            pre[px, pl.ds(pl.multiple_of(t * 64 + h * 32, 32), 32), :] = out[:, h * 128:(h + 1) * 128]
            start = pl.multiple_of(16 + t * 64 + h * 32, 16)
            act[px + 1, pl.ds(start, 32), :] = acts[:, h * 128:(h + 1) * 128]

    def conv_edge(px):
        cols = jnp.concatenate([a1[2 * px + k, 0:80, :] for k in range(3)], axis=0)
        out = (mm(w1, cols) + b1)[0:16]
        acts = (out * sigmoid(out)).astype(BF)
        act[px + 1, 0:16, :] = jnp.where(my == 0, jnp.zeros_like(acts), acts)

    def conv_high_1(t, carry):
        conv_high(1, t)
        return carry

    def conv_high_0(t, carry):
        conv_high(0, t)
        return carry

    def to_taps(xs, first, count):
        low = act[xs, pl.ds(pl.multiple_of(16 * first, 16), 16 * count), :]
        high = act[xs, pl.ds(pl.multiple_of(256 + 16 * first, 16), 16 * count), :]
        d = mm(jnp.concatenate([low, high], axis=1), tb[:, 0:384]).astype(BF)
        for t in range(count):
            for k in range(3):
                row = pl.multiple_of(((first + t) * 3 + k) * 16, 16)
                taps[xs, pl.ds(row, 16), :] = d[16 * t:16 * (t + 1), 128 * k:128 * (k + 1)]

    def all_taps(xs):
        def body(t, carry):
            to_taps(xs, 1 + 4 * t, 4)
            return carry

        lax.fori_loop(0, 4, body, 0, unroll=UNROLL[3])
        to_taps(xs, 0, 1)

    lax.fori_loop(1, 8, conv_high_1, 0, unroll=UNROLL[1])
    c_ax = [send(3, act.at[2, pl.ds(80, 448)], act.at[0, pl.ds(80, 448)], xu)]
    c_a1y.wait_recv()

    @pl.when(my == 0)
    def _():
        a1[1:5, 0:48, :] = jnp.zeros((4, 48, 128), BF)

    conv_high(1, 0)
    conv_edge(1)
    c_ax.append(send(4, act.at[2, pl.ds(0, 80)], act.at[0, pl.ds(0, 80)], xu))
    all_taps(2)
    c_a1c.wait_recv()

    @pl.when(jnp.logical_or(first_x, my == 0))
    def _():
        a1[0, 0:48, :] = jnp.zeros((48, 128), BF)

    for n in range(2):
        c_raw[n].wait_recv()

        @pl.when(first_x)
        def _():
            halo[:, 32 * n:32 * n + 32, :] = jnp.zeros((4, 32, 256), BF)

        def load(b):
            return halo[:, 16 * b:16 * b + 16, :]

        to_channels(load, 0, n)
        lax.fori_loop(4 * n, 4 * n + 4, conv_high_0, 0, unroll=UNROLL[1])
    conv_edge(0)
    all_taps(1)
    for copy in c_ax:
        copy.wait_recv()

    @pl.when(first_x)
    def _():
        act[0] = jnp.zeros((528, 128), BF)

    all_taps(0)

    def window(j):
        start = pl.multiple_of(j * 96, 16)
        return jnp.concatenate([taps[k, pl.ds(start, 144), :] for k in range(3)], axis=0)

    def conv_low(t, total):
        out = mm(wl[...], jnp.concatenate([window(2 * t), window(2 * t + 1)], axis=1)) + bl
        sig = sigmoid(out)
        slopes = (sig * (1.0 + out * (1.0 - sig))).astype(BF)
        values = out * sig
        for h in range(2):
            slope[0, pl.ds(pl.multiple_of(t * 64 + h * 32, 32), 32), :] = slopes[:, h * 128:(h + 1) * 128]
        return total + values[:, :128] + values[:, 128:]

    total = lax.fori_loop(0, 4, conv_low, jnp.zeros((32, 128), F32), unroll=UNROLL[4])

    lane = lax.broadcasted_iota(jnp.int32, (32, 128), 1)
    row = lax.broadcasted_iota(jnp.int32, (32, 128), 0)
    sums = jnp.sum(total, axis=1, keepdims=True)
    mine = jnp.broadcast_to(jnp.sum(jnp.where(lane == row, sums, 0.0), axis=0, keepdims=True), (8, 128))
    pool_s[0] = mine
    pool_1[mx] = mine
    line_1, line_2 = pool_1.at[:, pl.ds(0, 1)], pool_2.at[:, pl.ds(0, 1)]
    spread(0, mx, columns, line_1, lambda peer: pool_s.at[0, pl.ds(0, 1)])

    c_sx = send(6, slope.at[0], slope.at[1], xd)
    c_sy = send(7, slope.at[0, pl.ds(0, 32)], slope_y.at[0], {"gy": yd})
    c_sc = send(8, slope.at[0, pl.ds(0, 32)], slope_y.at[1], {**xd, "gy": yd})

    def low_back(t, carry):
        g, gb = carry
        us, ws = [], []
        for h in range(2):
            u = slope[0, pl.ds(pl.multiple_of(t * 64 + h * 32, 32), 32), :]
            us.append(u)
            ws.append(window(2 * t + h))
            gb = gb + u.astype(F32)
        g = g + mm_nt(jnp.concatenate(us, axis=1), jnp.concatenate(ws, axis=1))
        return g, gb

    g_low, gb_low = lax.fori_loop(
        0, 4, low_back, (jnp.zeros((32, 432), F32), jnp.zeros((32, 128), F32)), unroll=UNROLL[5]
    )
    last = jnp.concatenate(
        [g_low[:, 384:432], jnp.sum(gb_low, axis=1, keepdims=True), jnp.zeros((32, 79), F32)], axis=1
    )
    blocks = [g_low[:, 0:128], g_low[:, 128:256], g_low[:, 256:384], last]
    for b in range(4):
        for c in range(4):
            gsend[b * 4 + c] = blocks[c][8 * b:8 * (b + 1), :]
    per = 16 // nx
    g_1[mx] = gsend[pl.ds(mx * per, per)]
    spread(1, mx, columns, g_1, lambda peer: gsend.at[pl.ds(peer * per, per)])

    def spread_rows(px, t):
        u = slope[px, pl.ds(pl.multiple_of(t * 32, 32), 32), :]
        for h in range(2):
            d = mm(u, tb[128 * h:128 * (h + 1), 640:1024]).astype(BF)
            for k in range(3):
                start = pl.multiple_of(((8 * h + t) * 3 + k) * 32, 32)
                up[px, pl.ds(start, 32), :] = d[:, k * 128:(k + 1) * 128]

    def spread_own(t, carry):
        spread_rows(0, t)
        return carry

    def spread_halo(t, carry):
        spread_rows(1, t)
        return carry

    lax.fori_loop(0, 8, spread_own, 0, unroll=UNROLL[6])

    arrive(0, line_1, nx)
    part = add_up(pool_1, nx)
    pool_s[1] = part
    pool_2[mg] = part
    spread(2, mg, members, line_2, lambda peer: pool_s.at[1, pl.ds(0, 1)])

    c_sx.wait_recv()
    c_sy.wait_recv()
    c_sc.wait_recv()

    @pl.when(last_x)
    def _():
        slope[1] = jnp.zeros((256, 128), BF)
        slope_y[1] = jnp.zeros((32, 128), BF)

    @pl.when(my == ny - 1)
    def _():
        slope_y[...] = jnp.zeros((2, 32, 128), BF)

    lax.fori_loop(0, 8, spread_halo, 0, unroll=UNROLL[6])
    for px in range(2):
        d = mm(slope_y[px], tb[0:128, 640:1024]).astype(BF)
        for k in range(3):
            up[px, (48 + k) * 32:(49 + k) * 32, :] = d[:, k * 128:(k + 1) * 128]

    def slope_high(t, carry):
        px, yp = t // 8, lax.rem(t, 8)
        at = pl.ds(pl.multiple_of(yp * 64, 64), 64)
        val = pre[px, at, :]
        sig = sigmoid(val)
        pre[px, at, :] = sig * (1.0 + val * (1.0 - sig))
        return carry

    lax.fori_loop(0, 16, slope_high, 0, unroll=UNROLL[7])

    wb[...] = jnp.zeros_like(wb)
    for kx in range(3):
        for ky in range(3):
            for kz in range(3):
                r = (2 * (kx != 1) + (ky != 1)) * 16
                c = (2 * (kx == 0) + (ky == 0)) * 96 + kz * 32
                t = ((kx * 3 + ky) * 3 + kz) * 16
                wb[r:r + 16, c:c + 32] = wlt[t:t + 16, :]

    arrive(1, g_1, nx)
    part = add_up(g_1, nx)
    g_2s[...] = part
    g_2[mg] = part
    spread(3, mg, members, g_2, lambda peer: g_2s)

    offset, wanted = to_column(hb_row[...]), to_column(tg_row[...])
    arrive(2, line_2, group)
    part = add_up(pool_2, group)
    scale = 1.0 / cells
    pooled = part[0:1, 0:32] * scale
    weight = hw[...]
    predicted = jnp.sum(weight * pooled, axis=1, keepdims=True) + offset
    error = predicted - wanted
    signal = jnp.sum(weight * error, axis=0, keepdims=True)
    head_out[...] = error * pooled
    pred_out[...] = jnp.sum(jnp.where(eye(4), predicted, 0.0), axis=0, keepdims=True)
    weights = (wb[...].astype(F32) * jnp.concatenate([signal] * 12, axis=1)).astype(BF)

    def high_back(t, carry):
        g, gb = carry
        cols = []
        for h in range(2):
            start = pl.multiple_of(t * 192 + h * 96, 32)
            cols.append(jnp.concatenate([up[0, pl.ds(start, 192), :], up[1, pl.ds(start, 192), :]], axis=0))
        out = mm(weights, jnp.concatenate(cols, axis=1)).astype(BF)
        ws, ups = [], []
        for h in range(2):
            at = pl.ds(pl.multiple_of(t * 64 + h * 32, 32), 32)
            begin = pl.multiple_of(32 + t * 128 + h * 64, 16)
            for qx in range(2):
                tile = out[32 * qx:32 * (qx + 1), h * 128:(h + 1) * 128]
                grad_b[qx, at, :] = tile
                u = (tile.astype(F32) * pre[qx, at, :]).astype(BF)
                gb = gb + u.astype(F32)
                ups.append(u)
                ws.append(jnp.concatenate([a1[2 * qx + k, pl.ds(begin, 80), :] for k in range(3)], axis=0))
        g = g + mm_nt(jnp.concatenate(ups, axis=1), jnp.concatenate(ws, axis=1))
        return g, gb

    g_high, gb_high = lax.fori_loop(
        0, 8, high_back, (jnp.zeros((32, 240), F32), jnp.zeros((32, 128), F32)), unroll=UNROLL[8]
    )
    g_w = select(g_high[0:16], ta[0:240, 640:768]) + select(g_high[16:32], ta[0:240, 768:896])
    bias = jnp.sum(gb_high, axis=1, keepdims=True)
    lane16 = lax.broadcasted_iota(jnp.int32, (16, 128), 1)
    h_mine = jnp.where(lane16 == 108, bias[0:16] + bias[16:32], g_w) * scale
    h_s[0] = h_mine
    h_1[mx] = h_mine
    spread(4, mx, columns, h_1, lambda peer: h_s.at[0])

    arrive(3, g_2, group)
    part = add_up(g_2, group)
    g_3[mx] = part
    spread(5, mx, columns, g_3, lambda peer: g_3.at[mx])

    def place(t, carry):
        qx = t // 2
        h = lax.rem(t, 2)
        block = grad_b[qx, pl.ds(pl.multiple_of(h * 256, 256), 256), :]
        out = mm(tb[:, 384:640], block).astype(BF).reshape(16, 16, 128)
        bg_out[:, 2 * sg + qx, pl.ds(pl.multiple_of(h * 16, 16), 16), :] = out
        return carry

    lax.fori_loop(0, 4, place, 0, unroll=UNROLL[9])
    half = bg_out.at[:, pl.ds(2 * sg, 2)]
    c_bg = send(9, half, half, {"segment": 1 - sg})

    arrive(4, h_1, nx)
    part = add_up(h_1, nx)
    h_s[1] = part
    h_2[mg] = part
    spread(6, mg, members, h_2, lambda peer: h_s.at[1])

    arrive(5, g_3, nx)
    bands = []
    for b in range(4):
        bands.append(jnp.concatenate([g_3[(b * 4 + c) // per, (b * 4 + c) % per] for c in range(4)], axis=1))
    g_all = jnp.transpose(jnp.concatenate(bands, axis=0)) * (signal * scale)
    low_out[...] = g_all[0:432, :]
    low_bias[...] = g_all[432:433, :]
    moves = [deliver(n, ref) for n, ref in ((3, low_out), (4, low_bias), (2, head_out), (1, pred_out))]
    c_bg.wait_recv()
    moves.append(deliver(0, bg_out))

    arrive(6, h_2, group)
    h_tall[...] = jnp.transpose(add_up(h_2, group))
    for t in range(27):
        high_out[t] = h_tall[4 * t:4 * t + 4, :]
    high_bias[...] = h_tall[108:109, :]
    moves += [deliver(5, high_out), deliver(6, high_bias)]
    for copy in copies:
        copy.wait_send()
    for stage, buffer, n in stages:
        ref = buffer.at[pl.ds(0, n - 1)]
        pltpu.make_async_copy(ref, ref, ss.at[stage]).wait()
    for move in moves:
        move.wait()


def finish(*refs):
    sources, results, held, come, go = refs[:7], refs[7:14], refs[14:21], refs[21], refs[22]
    chain = [(sources[n], held[n], results[n]) for n in range(1, 7)]
    for n in range(4):
        chain.append([r.at[pl.ds(4 * n, 4)] for r in (sources[0], held[0], results[0])])
    loads = [pltpu.make_async_copy(x, y, come.at[n]) for n, (x, y, _) in enumerate(chain)]
    stores = [pltpu.make_async_copy(y, z, go.at[n]) for n, (_, y, z) in enumerate(chain)]
    for load in loads:
        load.start()
    for load, store in zip(loads, stores):
        load.wait()
        store.start()
    for store in stores:
        store.wait()


def shards(nx, ny, volume, weight_high, bias_high, weight_low, bias_low, head_weight, head_bias, targets):
    cells = 2 * nx * 16 * ny * 64
    small = (
        jnp.transpose(weight_high, (2, 3, 4, 1, 0)).reshape(27, 4, 16),
        jnp.transpose(weight_low, (2, 3, 4, 1, 0)).reshape(432, 32),
        bias_high[None],
        bias_low[None],
        head_weight.T,
        head_bias[None],
        targets[None],
    )
    tables = [jnp.asarray(t(), BF) for t in (early_tables, late_tables)]
    hbm = pl.BlockSpec(memory_space=pltpu.HBM)
    dma = pltpu.SemaphoreType.DMA
    per = 16 // nx
    group = 2 * ny
    results = (
        jax.ShapeDtypeStruct((16, 4, 32, 128), BF),
        jax.ShapeDtypeStruct((1, 4), F32),
        jax.ShapeDtypeStruct((4, 32), F32),
        jax.ShapeDtypeStruct((432, 32), F32),
        jax.ShapeDtypeStruct((1, 32), F32),
        jax.ShapeDtypeStruct((27, 4, 16), F32),
        jax.ShapeDtypeStruct((1, 16), F32),
    )
    outs = pl.pallas_call(
        functools.partial(kernel, nx, ny, cells),
        out_shape=results,
        in_specs=[hbm] * 10,
        out_specs=(hbm,) * 7,
        scratch_shapes=[
            *(pltpu.VMEM(a.shape, a.dtype) for a in results),
            pltpu.VMEM((4, 4, 64, 256), BF),
            pltpu.VMEM((256, 896), BF),
            pltpu.VMEM((256, 1024), BF),
            *(pltpu.VMEM(a.shape, a.dtype) for a in small),
            pltpu.VMEM((128, 16), F32),
            pltpu.VMEM((32, 432), BF),
            pltpu.VMEM((64, 384), BF),
            pltpu.VMEM((128, 16), F32),
            dma((10,)),
            dma((7,)),
            pltpu.VMEM((4, 64, 256), BF),
            pltpu.VMEM((5, 1072, 128), BF),
            pltpu.VMEM((2, 512, 128), F32),
            pltpu.VMEM((3, 528, 128), BF),
            pltpu.VMEM((3, 816, 128), BF),
            pltpu.VMEM((2, 256, 128), BF),
            pltpu.VMEM((2, 32, 128), BF),
            pltpu.VMEM((2, 1632, 128), BF),
            pltpu.VMEM((2, 512, 128), BF),
            pltpu.VMEM((2, 8, 128), F32),
            pltpu.VMEM((nx, 8, 128), F32),
            pltpu.VMEM((group, 8, 128), F32),
            pltpu.VMEM((16, 8, 128), F32),
            pltpu.VMEM((nx, per, 8, 128), F32),
            pltpu.VMEM((per, 8, 128), F32),
            pltpu.VMEM((group, per, 8, 128), F32),
            pltpu.VMEM((nx, per, 8, 128), F32),
            pltpu.VMEM((2, 16, 128), F32),
            pltpu.VMEM((nx, 16, 128), F32),
            pltpu.VMEM((group, 16, 128), F32),
            dma((10,)), dma((10,)), dma((7,)), dma((7,)),
        ],
        compiler_params=pltpu.CompilerParams(
            collective_id=0, has_side_effects=True, vmem_limit_bytes=64 << 20
        ),
        name="fused",
    )(volume, *tables, *small)
    bg, pred, head, low, low_bias, high, high_bias = pl.pallas_call(
        finish,
        out_shape=results,
        in_specs=[hbm] * 7,
        out_specs=(hbm,) * 7,
        scratch_shapes=[*(pltpu.VMEM(x.shape, x.dtype) for x in results), dma((10,)), dma((10,))],
        compiler_params=pltpu.CompilerParams(vmem_limit_bytes=64 << 20),
        name="finish",
    )(*outs)
    return (
        pred[0],
        bg,
        jnp.transpose(high.reshape(3, 3, 3, 4, 16), (4, 3, 0, 1, 2)),
        high_bias[0],
        jnp.transpose(low.reshape(3, 3, 3, 16, 32), (4, 3, 0, 1, 2)),
        low_bias[0],
        head.T,
    )


def solution(mesh):
    nx, ny = mesh.shape["gx"], mesh.shape["gy"]
    placed = (P(None, "gx", "gy", None), P(), P(), P(), P(), P(), P(), P())
    return jax.shard_map(
        functools.partial(shards, nx, ny),
        mesh=mesh,
        in_specs=placed,
        out_specs=(P(), P(None, "gx", "gy", None), P(), P(), P(), P(), P()),
        check_vma=False,
    )
```

```python
import functools

import jax
import jax.numpy as jnp
import numpy as np
from jax import lax
from jax.experimental import pallas as pl
from jax.experimental.pallas import tpu as pltpu
from jax.sharding import PartitionSpec as P

MESH = pl.DeviceIdType.MESH
BF = jnp.bfloat16
F32 = jnp.float32
UNROLL = (8, 4, 1, 4, 4, 4, 4, 4, 8, 4)


def depth_taps():
    z = np.arange(256)[:, None, None]
    k = np.arange(3)[None, :, None]
    p = np.arange(128)[None, None, :]
    return (z == 2 * p + k - 1).reshape(256, 384)


def rows_to_channels():
    out = np.zeros((16, 16, 12, 16), bool)
    for r in range(12):
        for y in range(16):
            out[y, r, r, y] = True
    return out.reshape(256, 192)


def depth_taps_low():
    out = np.zeros((2, 128, 3, 2, 64), bool)
    for h in range(2):
        for k in range(3):
            for p in range(64):
                if 2 * p + k - 1 >= 0:
                    out[h, 2 * p + k - 1, k, h, p] = True
    return out.reshape(256, 384)


def depth_spread():
    out = np.zeros((2, 64, 2, 3, 128), bool)
    for h in range(2):
        for k in range(3):
            for p in range(64):
                if 2 * p + k - 1 >= 0:
                    out[h, p, h, k, 2 * p + k - 1] = True
    return out.reshape(128, 768)


def channels_to_rows():
    out = np.zeros((16, 16, 16, 16), bool)
    for i in range(16):
        for y in range(16):
            out[i, y, y, i] = True
    return out.reshape(256, 256)


def high_order():
    out = np.zeros((2, 3, 5, 16, 128), bool)
    for s in range(2):
        for kx in range(3):
            for ky in range(3):
                for kz in range(3):
                    for c in range(4):
                        out[s, kx, ky + 2 * s, kz * 4 + c, ((kx * 3 + ky) * 3 + kz) * 4 + c] = True
    return out.reshape(2, 240, 128)


def early_tables():
    out = np.zeros((256, 896), np.float32)
    out[:, 0:384] = depth_taps()
    out[:, 384:576] = rows_to_channels()
    out[0:240, 640:768], out[0:240, 768:896] = high_order()
    return out


def late_tables():
    out = np.zeros((256, 1024), np.float32)
    out[:, 0:384] = depth_taps_low()
    out[:, 384:640] = channels_to_rows()
    spread = depth_spread()
    out[0:128, 640:1024] = spread[:, 0:384]
    out[128:256, 640:1024] = spread[:, 384:768]
    return out


def mm(a, b):
    return lax.dot_general(a, b, (((1,), (0,)), ((), ())), preferred_element_type=F32)


def mm_nt(a, b):
    return lax.dot_general(a, b, (((1,), (1,)), ((), ())), preferred_element_type=F32)


def thirds(x):
    a = x.astype(BF)
    rest = x - a.astype(F32)
    b = rest.astype(BF)
    c = (rest - b.astype(F32)).astype(BF)
    return jnp.concatenate([a, b, c], axis=0)


def select(x, table):
    n = x.shape[0]
    out = mm(thirds(x), table)
    return out[0:n] + out[n:2 * n] + out[2 * n:3 * n]


def sigmoid(x):
    return jax.nn.sigmoid(x)


def kernel(
    nx, ny, cells,
    v_hbm, ta_hbm, tb_hbm, *rest,
):
    small_hbm, results, rest = rest[:7], rest[7:14], rest[14:]
    (
        bg_out, pred_out, head_out, low_out, low_bias, high_out, high_bias,
        v, ta, tb, wh, wlt, bh_row, bl_row, hw, hb_row, tg_row,
        w_tall, wl, wb, h_tall, ls, os,
        halo, a1, pre, act, taps, slope, slope_y, up, grad_b,
        pool_s, pool_1, pool_2, gsend, g_1, g_2s, g_2, g_3, h_s, h_1, h_2,
        hs, hr, ss, rs,
    ) = rest
    sg = lax.axis_index("segment")
    mx = lax.axis_index("gx")
    my = lax.axis_index("gy")
    group = 2 * ny
    mg = sg * ny + my
    yu, yd = lax.rem(my + 1, ny), lax.rem(my + ny - 1, ny)
    xu = {"segment": 1 - sg, "gx": lax.rem(mx + sg, nx)}
    xd = {"segment": 1 - sg, "gx": lax.rem(mx + nx - 1 + sg, nx)}
    first_x = jnp.logical_and(mx == 0, sg == 0)
    last_x = jnp.logical_and(mx == nx - 1, sg == 1)

    loads = [
        pltpu.make_async_copy(v_hbm.at[:, pl.ds(4 * sg, 4)], v, ls.at[0]),
        pltpu.make_async_copy(ta_hbm, ta, ls.at[1]),
    ]
    for n, (src, dst) in enumerate(zip(small_hbm, (wh, wlt, bh_row, bl_row, hw, hb_row, tg_row))):
        loads.append(pltpu.make_async_copy(src, dst, ls.at[2 + n]))
    loads.append(pltpu.make_async_copy(tb_hbm, tb, ls.at[9]))
    for load in loads:
        load.start()

    columns, members = [], []
    if nx == 16:
        far = [(a, b) for a in range(4) for b in range(4) if a or b]
        far.sort(key=lambda t: -min(t[0], 4 - t[0]) - min(t[1], 4 - t[1]))
        for a, b in far:
            at = lax.rem(mx // 4 + a, 4) * 4 + lax.rem(lax.rem(mx, 4) + b, 4)
            columns.append((at, {"gx": at}))
    else:
        for d in range(1, nx):
            at = lax.rem(mx + d, nx)
            columns.append((at, {"gx": at}))
    far = [(a, b) for a in range(2) for b in range(ny) if a or b]
    far.sort(key=lambda t: -min(t[1], ny - t[1]))
    for a, b in far:
        seg = 1 - sg if a else sg
        at = lax.rem(my + b, ny)
        members.append((seg * ny + at, {"segment": seg, "gy": at}))

    barrier = pltpu.get_barrier_semaphore()
    partners = [peer for _, peer in members + columns]
    partners += [xu, xd, {**xu, "gy": yu}, {**xd, "gy": yd}]
    for peer in partners:
        pl.semaphore_signal(barrier, inc=1, device_id=peer, device_id_type=MESH)

    def deliver(n, ref):
        move = pltpu.make_async_copy(ref, results[n], os.at[n])
        move.start()
        return move

    copies = []

    def send(n, src, dst, peer):
        copy = pltpu.make_async_remote_copy(
            src_ref=src, dst_ref=dst, send_sem=hs.at[n], recv_sem=hr.at[n],
            device_id=peer, device_id_type=MESH,
        )
        copy.start()
        copies.append(copy)
        return copy

    stages = []

    def spread(stage, me, peers, buffer, source):
        for at, peer in peers:
            pltpu.make_async_remote_copy(
                src_ref=source(at), dst_ref=buffer.at[me],
                send_sem=ss.at[stage], recv_sem=rs.at[stage],
                device_id=peer, device_id_type=MESH,
            ).start()
        stages.append((stage, buffer, len(peers) + 1))

    def arrive(stage, buffer, n):
        ref = buffer.at[pl.ds(0, n - 1)]
        pltpu.make_async_copy(ref, ref, rs.at[stage]).wait()

    def add_up(buffer, n):
        part = buffer[0]
        for d in range(1, n):
            part = part + buffer[d]
        return part

    def to_channels(rows, xs, first):
        count = rows.shape[1] // 16
        d = mm(rows.reshape(64 * count, 256), ta[:, 0:384]).astype(BF)
        parts = []
        for h in range(count):
            at = [16 * (c * count + h) for c in range(4)]
            parts.append(
                jnp.concatenate([d[r:r + 16, 128 * k:128 * (k + 1)] for k in range(3) for r in at], axis=0)
            )
        out = mm(ta[:, 384:576], jnp.concatenate(parts, axis=1)).astype(BF)
        for h in range(count):
            start = pl.multiple_of(48 + (first + h) * 256, 16)
            a1[xs, pl.ds(start, 256), :] = out[:, h * 128:(h + 1) * 128]

    def own_plane(t, carry):
        to_channels(v[:, t], t + 1, 0)
        return carry

    loads[0].wait()
    loads[1].wait()
    lax.fori_loop(0, 4, own_plane, 0, unroll=4)

    pl.semaphore_wait(barrier, len(partners))

    c_raw = [
        send(5 * n, v.at[:, 3, pl.ds(32 * n, 32)], halo.at[:, pl.ds(32 * n, 32)], xu) for n in range(2)
    ]
    c_a1y = send(1, a1.at[pl.ds(1, 4), pl.ds(1024, 48)], a1.at[pl.ds(1, 4), pl.ds(0, 48)], {"gy": yu})
    c_a1c = send(2, a1.at[4, pl.ds(1024, 48)], a1.at[0, pl.ds(0, 48)], {**xu, "gy": yu})

    for load in loads[2:]:
        load.wait()

    def eye(n):
        r = lax.broadcasted_iota(jnp.int32, (n, n), 0)
        return r == lax.broadcasted_iota(jnp.int32, (n, n), 1)

    def to_column(row):
        n = row.shape[1]
        return jnp.sum(jnp.where(eye(n), row, 0.0), axis=1, keepdims=True)

    w_tall[...] = jnp.zeros_like(w_tall)
    for t in range(27):
        w_tall[4 * t:4 * t + 4, :] = wh[t].astype(F32)
    w_flat = mm_nt(eye(16).astype(F32).astype(BF), w_tall[...].astype(BF)).astype(BF)
    w1 = jnp.concatenate(
        [mm_nt(w_flat, ta[0:240, 640:768]), mm_nt(w_flat, ta[0:240, 768:896])], axis=0
    ).astype(BF)
    wl[...] = mm_nt(eye(32).astype(F32).astype(BF), wlt[...]).astype(BF)
    b1 = to_column(bh_row[...])
    b1 = jnp.concatenate([b1, b1], axis=0)
    bl = to_column(bl_row[...])

    def conv_high(px, t):
        cols = []
        for h in range(2):
            start = pl.multiple_of(32 + t * 128 + h * 64, 16)
            cols.append(jnp.concatenate([a1[2 * px + k, pl.ds(start, 80), :] for k in range(3)], axis=0))
        out = mm(w1, jnp.concatenate(cols, axis=1)) + b1
        acts = (out * sigmoid(out)).astype(BF)
        for h in range(2):
            pre[px, pl.ds(pl.multiple_of(t * 64 + h * 32, 32), 32), :] = out[:, h * 128:(h + 1) * 128]
            start = pl.multiple_of(16 + t * 64 + h * 32, 16)
            act[px + 1, pl.ds(start, 32), :] = acts[:, h * 128:(h + 1) * 128]

    def conv_edge(px):
        cols = jnp.concatenate([a1[2 * px + k, 0:80, :] for k in range(3)], axis=0)
        out = (mm(w1, cols) + b1)[0:16]
        acts = (out * sigmoid(out)).astype(BF)
        act[px + 1, 0:16, :] = jnp.where(my == 0, jnp.zeros_like(acts), acts)

    def conv_high_1(t, carry):
        conv_high(1, t)
        return carry

    def conv_high_0(t, carry):
        conv_high(0, t)
        return carry

    def to_taps(xs, first, count):
        low = act[xs, pl.ds(pl.multiple_of(16 * first, 16), 16 * count), :]
        high = act[xs, pl.ds(pl.multiple_of(256 + 16 * first, 16), 16 * count), :]
        d = mm(jnp.concatenate([low, high], axis=1), tb[:, 0:384]).astype(BF)
        for t in range(count):
            for k in range(3):
                row = pl.multiple_of(((first + t) * 3 + k) * 16, 16)
                taps[xs, pl.ds(row, 16), :] = d[16 * t:16 * (t + 1), 128 * k:128 * (k + 1)]

    def all_taps(xs):
        def body(t, carry):
            to_taps(xs, 1 + 4 * t, 4)
            return carry

        lax.fori_loop(0, 4, body, 0, unroll=UNROLL[3])
        to_taps(xs, 0, 1)

    lax.fori_loop(1, 8, conv_high_1, 0, unroll=UNROLL[1])
    c_ax = [send(3, act.at[2, pl.ds(80, 448)], act.at[0, pl.ds(80, 448)], xu)]
    c_a1y.wait_recv()

    @pl.when(my == 0)
    def _():
        a1[1:5, 0:48, :] = jnp.zeros((4, 48, 128), BF)

    conv_high(1, 0)
    conv_edge(1)
    c_ax.append(send(4, act.at[2, pl.ds(0, 80)], act.at[0, pl.ds(0, 80)], xu))
    all_taps(2)
    c_a1c.wait_recv()

    @pl.when(jnp.logical_or(first_x, my == 0))
    def _():
        a1[0, 0:48, :] = jnp.zeros((48, 128), BF)

    for n in range(2):
        c_raw[n].wait_recv()

        @pl.when(first_x)
        def _():
            halo[:, 32 * n:32 * n + 32, :] = jnp.zeros((4, 32, 256), BF)

        to_channels(halo[:, 32 * n:32 * n + 32, :], 0, 2 * n)
        lax.fori_loop(4 * n, 4 * n + 4, conv_high_0, 0, unroll=UNROLL[1])
    conv_edge(0)
    all_taps(1)
    for copy in c_ax:
        copy.wait_recv()

    @pl.when(first_x)
    def _():
        act[0] = jnp.zeros((528, 128), BF)

    all_taps(0)

    def window(j):
        start = pl.multiple_of(j * 96, 16)
        return jnp.concatenate([taps[k, pl.ds(start, 144), :] for k in range(3)], axis=0)

    def conv_low(t, total):
        out = mm(wl[...], jnp.concatenate([window(2 * t), window(2 * t + 1)], axis=1)) + bl
        sig = sigmoid(out)
        slopes = (sig * (1.0 + out * (1.0 - sig))).astype(BF)
        values = out * sig
        for h in range(2):
            slope[0, pl.ds(pl.multiple_of(t * 64 + h * 32, 32), 32), :] = slopes[:, h * 128:(h + 1) * 128]
        return total + values[:, :128] + values[:, 128:]

    total = lax.fori_loop(0, 4, conv_low, jnp.zeros((32, 128), F32), unroll=UNROLL[4])

    lane = lax.broadcasted_iota(jnp.int32, (32, 128), 1)
    row = lax.broadcasted_iota(jnp.int32, (32, 128), 0)
    sums = jnp.sum(total, axis=1, keepdims=True)
    mine = jnp.broadcast_to(jnp.sum(jnp.where(lane == row, sums, 0.0), axis=0, keepdims=True), (8, 128))
    pool_s[0] = mine
    pool_1[mx] = mine
    line_1, line_2 = pool_1.at[:, pl.ds(0, 1)], pool_2.at[:, pl.ds(0, 1)]
    spread(0, mx, columns, line_1, lambda peer: pool_s.at[0, pl.ds(0, 1)])

    c_sx = send(6, slope.at[0], slope.at[1], xd)
    c_sy = send(7, slope.at[0, pl.ds(0, 32)], slope_y.at[0], {"gy": yd})
    c_sc = send(8, slope.at[0, pl.ds(0, 32)], slope_y.at[1], {**xd, "gy": yd})

    def low_back(t, carry):
        g, gb = carry
        us, ws = [], []
        for h in range(2):
            u = slope[0, pl.ds(pl.multiple_of(t * 64 + h * 32, 32), 32), :]
            us.append(u)
            ws.append(window(2 * t + h))
            gb = gb + u.astype(F32)
        g = g + mm_nt(jnp.concatenate(us, axis=1), jnp.concatenate(ws, axis=1))
        return g, gb

    g_low, gb_low = lax.fori_loop(
        0, 4, low_back, (jnp.zeros((32, 432), F32), jnp.zeros((32, 128), F32)), unroll=UNROLL[5]
    )
    last = jnp.concatenate(
        [g_low[:, 384:432], jnp.sum(gb_low, axis=1, keepdims=True), jnp.zeros((32, 79), F32)], axis=1
    )
    blocks = [g_low[:, 0:128], g_low[:, 128:256], g_low[:, 256:384], last]
    for b in range(4):
        for c in range(4):
            gsend[b * 4 + c] = blocks[c][8 * b:8 * (b + 1), :]
    per = 16 // nx
    g_1[mx] = gsend[pl.ds(mx * per, per)]
    spread(1, mx, columns, g_1, lambda peer: gsend.at[pl.ds(peer * per, per)])

    def spread_rows(px, t):
        u = slope[px, pl.ds(pl.multiple_of(t * 32, 32), 32), :]
        for h in range(2):
            d = mm(u, tb[128 * h:128 * (h + 1), 640:1024]).astype(BF)
            for k in range(3):
                start = pl.multiple_of(((8 * h + t) * 3 + k) * 32, 32)
                up[px, pl.ds(start, 32), :] = d[:, k * 128:(k + 1) * 128]

    def spread_own(t, carry):
        spread_rows(0, t)
        return carry

    def spread_halo(t, carry):
        spread_rows(1, t)
        return carry

    lax.fori_loop(0, 8, spread_own, 0, unroll=UNROLL[6])

    arrive(0, line_1, nx)
    part = add_up(pool_1, nx)
    pool_s[1] = part
    pool_2[mg] = part
    spread(2, mg, members, line_2, lambda peer: pool_s.at[1, pl.ds(0, 1)])

    c_sx.wait_recv()
    c_sy.wait_recv()
    c_sc.wait_recv()

    @pl.when(last_x)
    def _():
        slope[1] = jnp.zeros((256, 128), BF)
        slope_y[1] = jnp.zeros((32, 128), BF)

    @pl.when(my == ny - 1)
    def _():
        slope_y[...] = jnp.zeros((2, 32, 128), BF)

    lax.fori_loop(0, 8, spread_halo, 0, unroll=UNROLL[6])
    for px in range(2):
        d = mm(slope_y[px], tb[0:128, 640:1024]).astype(BF)
        for k in range(3):
            up[px, (48 + k) * 32:(49 + k) * 32, :] = d[:, k * 128:(k + 1) * 128]

    def slope_high(t, carry):
        px, yp = t // 8, lax.rem(t, 8)
        at = pl.ds(pl.multiple_of(yp * 64, 64), 64)
        val = pre[px, at, :]
        sig = sigmoid(val)
        pre[px, at, :] = sig * (1.0 + val * (1.0 - sig))
        return carry

    lax.fori_loop(0, 16, slope_high, 0, unroll=UNROLL[7])

    wb[...] = jnp.zeros_like(wb)
    for kx in range(3):
        for ky in range(3):
            for kz in range(3):
                r = (2 * (kx != 1) + (ky != 1)) * 16
                c = (2 * (kx == 0) + (ky == 0)) * 96 + kz * 32
                t = ((kx * 3 + ky) * 3 + kz) * 16
                wb[r:r + 16, c:c + 32] = wlt[t:t + 16, :]

    arrive(1, g_1, nx)
    part = add_up(g_1, nx)
    g_2s[...] = part
    g_2[mg] = part
    spread(3, mg, members, g_2, lambda peer: g_2s)

    offset, wanted = to_column(hb_row[...]), to_column(tg_row[...])
    arrive(2, line_2, group)
    part = add_up(pool_2, group)
    scale = 1.0 / cells
    pooled = part[0:1, 0:32] * scale
    weight = hw[...]
    predicted = jnp.sum(weight * pooled, axis=1, keepdims=True) + offset
    error = predicted - wanted
    signal = jnp.sum(weight * error, axis=0, keepdims=True)
    head_out[...] = error * pooled
    pred_out[...] = jnp.sum(jnp.where(eye(4), predicted, 0.0), axis=0, keepdims=True)
    weights = (wb[...].astype(F32) * jnp.concatenate([signal] * 12, axis=1)).astype(BF)

    def high_back(t, carry):
        g, gb = carry
        cols = []
        for h in range(2):
            start = pl.multiple_of(t * 192 + h * 96, 32)
            cols.append(jnp.concatenate([up[0, pl.ds(start, 192), :], up[1, pl.ds(start, 192), :]], axis=0))
        out = mm(weights, jnp.concatenate(cols, axis=1)).astype(BF)
        ws, ups = [], []
        for h in range(2):
            at = pl.ds(pl.multiple_of(t * 64 + h * 32, 32), 32)
            begin = pl.multiple_of(32 + t * 128 + h * 64, 16)
            for qx in range(2):
                tile = out[32 * qx:32 * (qx + 1), h * 128:(h + 1) * 128]
                grad_b[qx, at, :] = tile
                u = (tile.astype(F32) * pre[qx, at, :]).astype(BF)
                gb = gb + u.astype(F32)
                ups.append(u)
                ws.append(jnp.concatenate([a1[2 * qx + k, pl.ds(begin, 80), :] for k in range(3)], axis=0))
        g = g + mm_nt(jnp.concatenate(ups, axis=1), jnp.concatenate(ws, axis=1))
        return g, gb

    g_high, gb_high = lax.fori_loop(
        0, 8, high_back, (jnp.zeros((32, 240), F32), jnp.zeros((32, 128), F32)), unroll=UNROLL[8]
    )
    g_w = select(g_high[0:16], ta[0:240, 640:768]) + select(g_high[16:32], ta[0:240, 768:896])
    bias = jnp.sum(gb_high, axis=1, keepdims=True)
    lane16 = lax.broadcasted_iota(jnp.int32, (16, 128), 1)
    h_mine = jnp.where(lane16 == 108, bias[0:16] + bias[16:32], g_w) * scale
    h_s[0] = h_mine
    h_1[mx] = h_mine
    spread(4, mx, columns, h_1, lambda peer: h_s.at[0])

    arrive(3, g_2, group)
    part = add_up(g_2, group)
    g_3[mx] = part
    spread(5, mx, columns, g_3, lambda peer: g_3.at[mx])

    def place(t, carry):
        qx = t // 2
        h = lax.rem(t, 2)
        block = grad_b[qx, pl.ds(pl.multiple_of(h * 256, 256), 256), :]
        out = mm(tb[:, 384:640], block).astype(BF).reshape(16, 16, 128)
        bg_out[:, 2 * sg + qx, pl.ds(pl.multiple_of(h * 16, 16), 16), :] = out
        return carry

    lax.fori_loop(0, 4, place, 0, unroll=UNROLL[9])
    half = bg_out.at[:, pl.ds(2 * sg, 2)]
    c_bg = send(9, half, half, {"segment": 1 - sg})

    arrive(4, h_1, nx)
    part = add_up(h_1, nx)
    h_s[1] = part
    h_2[mg] = part
    spread(6, mg, members, h_2, lambda peer: h_s.at[1])

    arrive(5, g_3, nx)
    bands = []
    for b in range(4):
        bands.append(jnp.concatenate([g_3[(b * 4 + c) // per, (b * 4 + c) % per] for c in range(4)], axis=1))
    g_all = jnp.transpose(jnp.concatenate(bands, axis=0)) * (signal * scale)
    low_out[...] = g_all[0:432, :]
    low_bias[...] = g_all[432:433, :]
    moves = [deliver(n, ref) for n, ref in ((3, low_out), (4, low_bias), (2, head_out), (1, pred_out))]
    c_bg.wait_recv()
    moves.append(deliver(0, bg_out))

    arrive(6, h_2, group)
    h_tall[...] = jnp.transpose(add_up(h_2, group))
    for t in range(27):
        high_out[t] = h_tall[4 * t:4 * t + 4, :]
    high_bias[...] = h_tall[108:109, :]
    moves += [deliver(5, high_out), deliver(6, high_bias)]
    for copy in copies:
        copy.wait_send()
    for stage, buffer, n in stages:
        ref = buffer.at[pl.ds(0, n - 1)]
        pltpu.make_async_copy(ref, ref, ss.at[stage]).wait()
    for move in moves:
        move.wait()


def finish(*refs):
    sources, results, held, come, go = refs[:7], refs[7:14], refs[14:21], refs[21], refs[22]
    chain = [(sources[n], held[n], results[n]) for n in range(1, 7)]
    for n in range(4):
        chain.append([r.at[pl.ds(4 * n, 4)] for r in (sources[0], held[0], results[0])])
    loads = [pltpu.make_async_copy(x, y, come.at[n]) for n, (x, y, _) in enumerate(chain)]
    stores = [pltpu.make_async_copy(y, z, go.at[n]) for n, (_, y, z) in enumerate(chain)]
    for load in loads:
        load.start()
    for load, store in zip(loads, stores):
        load.wait()
        store.start()
    for store in stores:
        store.wait()


def shards(nx, ny, volume, weight_high, bias_high, weight_low, bias_low, head_weight, head_bias, targets):
    cells = 2 * nx * 16 * ny * 64
    small = (
        jnp.transpose(weight_high, (2, 3, 4, 1, 0)).reshape(27, 4, 16),
        jnp.transpose(weight_low, (2, 3, 4, 1, 0)).reshape(432, 32),
        bias_high[None],
        bias_low[None],
        head_weight.T,
        head_bias[None],
        targets[None],
    )
    tables = [jnp.asarray(t(), BF) for t in (early_tables, late_tables)]
    hbm = pl.BlockSpec(memory_space=pltpu.HBM)
    dma = pltpu.SemaphoreType.DMA
    per = 16 // nx
    group = 2 * ny
    results = (
        jax.ShapeDtypeStruct((16, 4, 32, 128), BF),
        jax.ShapeDtypeStruct((1, 4), F32),
        jax.ShapeDtypeStruct((4, 32), F32),
        jax.ShapeDtypeStruct((432, 32), F32),
        jax.ShapeDtypeStruct((1, 32), F32),
        jax.ShapeDtypeStruct((27, 4, 16), F32),
        jax.ShapeDtypeStruct((1, 16), F32),
    )
    outs = pl.pallas_call(
        functools.partial(kernel, nx, ny, cells),
        out_shape=results,
        in_specs=[hbm] * 10,
        out_specs=(hbm,) * 7,
        scratch_shapes=[
            *(pltpu.VMEM(a.shape, a.dtype) for a in results),
            pltpu.VMEM((4, 4, 64, 256), BF),
            pltpu.VMEM((256, 896), BF),
            pltpu.VMEM((256, 1024), BF),
            *(pltpu.VMEM(a.shape, a.dtype) for a in small),
            pltpu.VMEM((128, 16), F32),
            pltpu.VMEM((32, 432), BF),
            pltpu.VMEM((64, 384), BF),
            pltpu.VMEM((128, 16), F32),
            dma((10,)),
            dma((7,)),
            pltpu.VMEM((4, 64, 256), BF),
            pltpu.VMEM((5, 1072, 128), BF),
            pltpu.VMEM((2, 512, 128), F32),
            pltpu.VMEM((3, 528, 128), BF),
            pltpu.VMEM((3, 816, 128), BF),
            pltpu.VMEM((2, 256, 128), BF),
            pltpu.VMEM((2, 32, 128), BF),
            pltpu.VMEM((2, 1632, 128), BF),
            pltpu.VMEM((2, 512, 128), BF),
            pltpu.VMEM((2, 8, 128), F32),
            pltpu.VMEM((nx, 8, 128), F32),
            pltpu.VMEM((group, 8, 128), F32),
            pltpu.VMEM((16, 8, 128), F32),
            pltpu.VMEM((nx, per, 8, 128), F32),
            pltpu.VMEM((per, 8, 128), F32),
            pltpu.VMEM((group, per, 8, 128), F32),
            pltpu.VMEM((nx, per, 8, 128), F32),
            pltpu.VMEM((2, 16, 128), F32),
            pltpu.VMEM((nx, 16, 128), F32),
            pltpu.VMEM((group, 16, 128), F32),
            dma((10,)), dma((10,)), dma((7,)), dma((7,)),
        ],
        compiler_params=pltpu.CompilerParams(
            collective_id=0, has_side_effects=True, vmem_limit_bytes=64 << 20
        ),
        name="fused",
    )(volume, *tables, *small)
    bg, pred, head, low, low_bias, high, high_bias = pl.pallas_call(
        finish,
        out_shape=results,
        in_specs=[hbm] * 7,
        out_specs=(hbm,) * 7,
        scratch_shapes=[*(pltpu.VMEM(x.shape, x.dtype) for x in results), dma((10,)), dma((10,))],
        compiler_params=pltpu.CompilerParams(vmem_limit_bytes=64 << 20),
        name="finish",
    )(*outs)
    return (
        pred[0],
        bg,
        jnp.transpose(high.reshape(3, 3, 3, 4, 16), (4, 3, 0, 1, 2)),
        high_bias[0],
        jnp.transpose(low.reshape(3, 3, 3, 16, 32), (4, 3, 0, 1, 2)),
        low_bias[0],
        head.T,
    )


def solution(mesh):
    nx, ny = mesh.shape["gx"], mesh.shape["gy"]
    placed = (P(None, "gx", "gy", None), P(), P(), P(), P(), P(), P(), P())
    return jax.shard_map(
        functools.partial(shards, nx, ny),
        mesh=mesh,
        in_specs=placed,
        out_specs=(P(), P(None, "gx", "gy", None), P(), P(), P(), P(), P()),
        check_vma=False,
    )
```
